256 devices in a mesh: px: 16 (over y, x), py: 16 (over z, core).
Axes of the slice: x: 4, y: 4, z: 8, core: 2. Of those that a mesh axis runs over, the one named last changes fastest.
Arguments:
- start_field: float32 [128, 256, 512], P('px', 'py'), may hold values from -1.7 to 1.7
- known: float32 [8, 128, 256, 512], P(None, 'px', 'py'), may hold values from -1 to 1
Outputs:
- solution_field: float32 [128, 256, 512], P('px', 'py')
- residual: float32 [128, 256, 512], P('px', 'py')
The draws below stay inside these ranges and needn't reach their ends.
All inputs are finite; a program needn't handle non-finite values.
Results may differ from the reference program's by a relative error of at most 0.01.
Values sent between devices are 32-bit elements; how exact they have to be, the bound alone decides.
No kernel may reach another device: no remote copies, remote signals or barrier semaphores. Data moves between devices by JAX's collectives and lax.ppermute only.
A program may use at most 64 MiB of HBM per device.

```python
import math
import jax
import jax.numpy as jnp
from jax import lax

NZ = 512
NKNOWN = 8
NEWTON = 2
ITERS = 3
NX = 128
NY = 256


def ramp_plane():
    xs = jnp.arange(NX, dtype=jnp.float32) / max(NX - 1, 1)
    ys = jnp.arange(NY, dtype=jnp.float32) / max(NY - 1, 1)
    return 0.5 * (xs[:, None] + ys[None, :])


def smooth_sum(key, count):
    freqs = jax.random.uniform(jax.random.fold_in(key, 1), (count, 4, 3), jnp.float32, 1.0, 6.0)
    phases = jax.random.uniform(jax.random.fold_in(key, 2), (count, 4, 3), jnp.float32, -math.pi, math.pi)
    weights = jax.random.uniform(jax.random.fold_in(key, 3), (count, 4), jnp.float32, 0.5, 1.0)
    weights = weights / jnp.sum(weights, axis=1, keepdims=True)
    xs = jnp.arange(NX, dtype=jnp.float32) / NX
    ys = jnp.arange(NY, dtype=jnp.float32) / NY
    zs = jnp.arange(NZ, dtype=jnp.float32) / NZ
    total = jnp.zeros((count, NX, NY, NZ), jnp.float32)
    for term in range(4):
        wave_x = jnp.cos(2.0 * math.pi * freqs[:, term, 0, None] * xs[None, :] + phases[:, term, 0, None])
        wave_y = jnp.cos(2.0 * math.pi * freqs[:, term, 1, None] * ys[None, :] + phases[:, term, 1, None])
        wave_z = jnp.cos(2.0 * math.pi * freqs[:, term, 2, None] * zs[None, :] + phases[:, term, 2, None])
        total = total + weights[:, term, None, None, None] * wave_x[:, :, None, None] * wave_y[:, None, :, None] * wave_z[:, None, None, :]
    return total


def known_fields(key):
    shape_sum = smooth_sum(jax.random.fold_in(key, 21), NKNOWN)
    sharpness = 3.0
    amplitude = 0.4 + 0.6 * ramp_plane()
    return amplitude[None, :, :, None] * jnp.tanh(sharpness * shape_sum)


def draw_known(key, part):
    return known_fields(key)


def draw_start_field(key, part):
    fields = known_fields(key)
    order = jax.random.permutation(jax.random.fold_in(key, 31), NKNOWN)
    mixing = jax.random.uniform(jax.random.fold_in(key, 32), (), jnp.float32, 0.55, 0.8)
    blend = mixing * fields[order[0]] + (1.0 - mixing) * fields[order[1]]
    smooth = smooth_sum(jax.random.fold_in(key, 33), 1)[0]
    rough = jax.random.uniform(jax.random.fold_in(key, 34), (NX, NY, NZ), jnp.float32, -1.0, 1.0)
    spread = (0.4 + 0.8 * ramp_plane())[:, :, None]
    return blend + spread * (0.2 * smooth + 0.25 * rough)


def setup_inputs(seed: int = 0) -> dict:
    key_list = jax.random.split(jax.random.key(seed), 3)
    start_field = draw_start_field(jax.random.fold_in(key_list[2], 71), 0)
    known = draw_known(jax.random.fold_in(key_list[2], 71), 0)
    return dict(start_field=start_field, known=known)


DIFFUSION = 0.5
SHIFT = 4.0
EPS = 1e-06

def laplace(field):
    padded = jnp.pad(field, 1)
    beside = padded[2:, 1:-1, 1:-1] + padded[:-2, 1:-1, 1:-1]
    beside = beside + padded[1:-1, 2:, 1:-1] + padded[1:-1, :-2, 1:-1]
    beside = beside + padded[1:-1, 1:-1, 2:] + padded[1:-1, 1:-1, :-2]
    return beside - 6.0 * field

def allen_cahn(field, lap):
    return DIFFUSION * lap + field - field * field * field

def solve_small(hess, beta):
    normal = lax.optimization_barrier(jnp.sum(hess[:, :, None] * hess[:, None, :], axis=0))
    target = beta * hess[0]
    lower = jnp.linalg.cholesky(normal)
    count = normal.shape[0]
    forward = []
    for i in range(count):
        acc = target[i]
        for j in range(i):
            acc = acc - lower[i, j] * forward[j]
        forward.append(acc / lower[i, i])
    back = [None] * count
    for i in reversed(range(count)):
        acc = forward[i]
        for j in range(i + 1, count):
            acc = acc - lower[j, i] * back[j]
        back[i] = acc / lower[i, i]
    return jnp.stack(back)

def reference(start_field, known):
    cells = float(NX * NY * NZ)
    field = start_field
    for step in range(NEWTON):
        force = allen_cahn(field, laplace(field))
        dist = jnp.stack([jnp.sum((field - known[i]) * (field - known[i])) for i in range(NKNOWN)])
        beta = jnp.sqrt(jnp.sum(force * force) + EPS)
        basis = [-force / beta]
        jac_diag = 1.0 - 3.0 * field * field
        hess = jnp.zeros((ITERS + 1, ITERS), jnp.float32)
        for k in range(ITERS):
            image = DIFFUSION * laplace(basis[k]) + jac_diag * basis[k]
            heights = jnp.stack([jnp.sum(vec * image) for vec in basis])
            rest = image
            for j in range(k + 1):
                rest = rest - heights[j] * basis[j]
            height = jnp.sqrt(jnp.sum(rest * rest) + EPS)
            hess = hess.at[:k + 1, k].set(heights).at[k + 1, k].set(height)
            if k < ITERS - 1:
                basis.append(rest / height)
        coeffs = solve_small(hess, beta)
        delta = coeffs[0] * basis[0]
        for j in range(1, ITERS):
            delta = delta + coeffs[j] * basis[j]
        inner = jnp.stack([jnp.sum((field - known[i]) * delta) for i in range(NKNOWN)])
        mean_dist = dist / cells + EPS
        weight = 1.0 / mean_dist + SHIFT
        total = jnp.sum(2.0 * inner / (cells * mean_dist * mean_dist * weight))
        scale = 1.0 / (1.0 + jnp.abs(total))
        field = field + scale * delta
    return (field, allen_cahn(field, laplace(field)))
```

```python
import jax
import jax.numpy as jnp
from jax import lax
from jax.experimental import pallas as pl
from jax.experimental.pallas import tpu as pltpu
from jax.sharding import PartitionSpec as P

EPS = 1e-06
DEFLATE = 4.0
ITERS = 3
KNOWN = 8
AXES = ("px", "py")
HX = 7
HY = 8
LANES = 128
F32 = jnp.float32

DIST, CROSS = 8, 16


def iotas():
    row = lax.broadcasted_iota(jnp.int32, (8, LANES), 0)
    lane = lax.broadcasted_iota(jnp.int32, (8, LANES), 1)
    return row, lane


def plane_sums(ref, x, tiles, ncol):
    row, lane = iotas()
    top = ref.shape[1] // 8
    zero = jnp.zeros((8, LANES), F32)
    need = range(max(tiles[0] - 1, 0), min(tiles[-1] + 2, top))
    v = {(t, c): ref[x, 8 * t:8 * t + 8, LANES * c:LANES * c + LANES] for t in need for c in range(ncol)}
    up = {(t, c): pltpu.roll(v[t, c], 1, 0) for t in need if t <= tiles[-1] for c in range(ncol)}
    down = {(t, c): pltpu.roll(v[t, c], 7, 0) for t in need if t >= tiles[0] for c in range(ncol)}
    out = {}
    for t in tiles:
        left = [pltpu.roll(v[t, c], 1, 1) for c in range(ncol)]
        right = [pltpu.roll(v[t, c], LANES - 1, 1) for c in range(ncol)]
        for c in range(ncol):
            rows, cols = slice(8 * t, 8 * t + 8), slice(LANES * c, LANES * c + LANES)
            a = up[t, c] if t == 0 else jnp.where(row == 0, up[t - 1, c], up[t, c])
            b = down[t, c] if t == top - 1 else jnp.where(row == 7, down[t + 1, c], down[t, c])
            l = jnp.where(lane == 0, left[c - 1] if c else zero, left[c])
            r = jnp.where(lane == LANES - 1, right[c + 1] if c < ncol - 1 else zero, right[c])
            total = (ref[x - 1, rows, cols] + ref[x + 1, rows, cols]) + (a + b) + (l + r)
            out[t, c] = (v[t, c], total)
    return out


def tile(t, c):
    return slice(8 * t, 8 * t + 8), slice(LANES * c, LANES * c + LANES)


def edges():
    ix, iy = lax.axis_index("px"), lax.axis_index("py")
    nx, ny = lax.axis_size("px"), lax.axis_size("py")
    flag = lambda cond: jnp.where(cond, 0.0, 1.0).astype(F32)
    return flag(ix == 0), flag(ix == nx - 1), flag(iy == 0), flag(iy == ny - 1)


def krylov(u_ref, w_refs, out_w, lo, hi, known_ref, sums_ref):
    ncol = u_ref.shape[2] // LANES
    planes = u_ref.shape[0]
    top = u_ref.shape[1] // 8
    x_lo, x_hi, y_lo, y_hi = edges()
    first, last = HX, planes - HX

    def mask(x):
        m = jnp.where(x < first, x_lo, jnp.where(x >= last, x_hi, 1.0))
        return m

    def stage(k):
        src = u_ref if k == 0 else w_refs[k - 1]
        dst = w_refs[k]

        def body(x, carry):
            m = mask(x)
            sums = plane_sums(src, x, list(range(top)), ncol)
            for (t, c), (v, total) in sums.items():
                rows, cols = tile(t, c)
                if k == 0:
                    value = 0.5 * total - v * (2.0 + v * v)
                else:
                    u = u_ref[x, rows, cols]
                    value = 0.5 * total + (1.0 - 3.0 * u * u) * v
                if t == 0:
                    value = value * (m * y_lo)
                elif t == top - 1:
                    value = value * (m * y_hi)
                else:
                    value = value * m
                dst[x, rows, cols] = value
            return carry

        lax.fori_loop(lo + k, hi - k, body, 0)

    for k in range(ITERS):
        stage(k)
    own = list(range(HY // 8, top - HY // 8))
    zero = jnp.zeros((8, LANES), F32)

    def moments(x, acc):
        acc = list(acc)
        sums = plane_sums(w_refs[2], x, own, ncol)
        for (t, c), (w2, total) in sums.items():
            rows, cols = tile(t, c)
            u = u_ref[x, rows, cols]
            w3 = 0.5 * total + (1.0 - 3.0 * u * u) * w2
            w0 = w_refs[0][x, rows, cols]
            w1 = w_refs[1][x, rows, cols]
            pairs = ((w0, w0), (w0, w1), (w1, w1), (w1, w2), (w2, w2), (w2, w3), (w3, w3))
            for n, (p, q) in enumerate(pairs):
                acc[n] = acc[n] + p * q
        return tuple(acc)

    acc = lax.fori_loop(first, last, moments, (zero,) * 7)

    def cross(x, acc):
        acc = list(acc)
        for t in own:
            for c in range(ncol):
                rows, cols = tile(t, c)
                u = u_ref[x, rows, cols]
                ws = [w_refs[m][x, rows, cols] for m in range(ITERS)]
                for i in range(KNOWN):
                    k = known_ref[i, x - first, slice(8 * t - HY, 8 * t - HY + 8), cols]
                    d = u - k
                    acc[i] = acc[i] + d * d
                    for m in range(ITERS):
                        acc[KNOWN * (m + 1) + i] = acc[KNOWN * (m + 1) + i] + d * ws[m]
        return tuple(acc)

    more = lax.fori_loop(first, last, cross, (zero,) * (KNOWN * (ITERS + 1)))
    parts = [jnp.sum(a, axis=0, keepdims=True) for a in (*acc, zero, *more)]
    block = jnp.concatenate(parts, axis=0)
    totals = jnp.sum(block, axis=1, keepdims=True)
    shape = block.shape
    hit = lax.broadcasted_iota(jnp.int32, shape, 0) == lax.broadcasted_iota(jnp.int32, shape, 1)
    line = jnp.sum(jnp.where(hit, totals, 0.0), axis=0, keepdims=True)
    sums_ref[...] = jnp.broadcast_to(line, sums_ref.shape)


def coefficients(recv_ref, cells):
    line = jnp.sum(recv_ref[...], axis=0, keepdims=True)
    line = jnp.broadcast_to(line, (8, LANES))
    mu = [jnp.broadcast_to(line[:, n:n + 1], (8, LANES)) for n in range(7)]
    zero = jnp.zeros((8, LANES), F32)

    def inner(p, q):
        total = None
        for i, a in enumerate(p):
            if a is None:
                continue
            part = None
            for j, b in enumerate(q):
                if b is None:
                    continue
                term = b * mu[i + j]
                part = term if part is None else part + term
            part = a * part
            total = part if total is None else total + part
        return total

    beta = jnp.sqrt(mu[0] + EPS)
    basis = [[-1.0 / beta]]
    hess = {}
    for k in range(ITERS):
        vec = basis[k]
        image = [None] * (k + 2)
        for i in range(k + 2):
            a = vec[i - 1] if i > 0 else None
            b = -3.0 * vec[i] if i <= k else None
            image[i] = b if a is None else (a if b is None else a + b)
        for j in range(k + 1):
            hess[j, k] = inner(basis[j], image)
        rest = list(image)
        for j in range(k + 1):
            for i in range(len(basis[j])):
                rest[i] = rest[i] - hess[j, k] * basis[j][i]
        square = jnp.maximum(inner(rest, rest), 0.0)
        hess[k + 1, k] = jnp.sqrt(square + EPS)
        if k < ITERS - 1:
            scale = 1.0 / hess[k + 1, k]
            basis.append([a * scale for a in rest])

    def normal(i, j):
        total = None
        for r in range(ITERS + 1):
            if (r, i) in hess and (r, j) in hess:
                term = hess[r, i] * hess[r, j]
                total = term if total is None else total + term
        return total

    lower = {}
    for j in range(ITERS):
        diag = normal(j, j)
        for r in range(j):
            diag = diag - lower[j, r] * lower[j, r]
        lower[j, j] = jnp.sqrt(diag)
        for i in range(j + 1, ITERS):
            off = normal(i, j)
            for r in range(j):
                off = off - lower[i, r] * lower[j, r]
            lower[i, j] = off / lower[j, j]
    forward = []
    for i in range(ITERS):
        part = beta * hess[0, i]
        for j in range(i):
            part = part - lower[i, j] * forward[j]
        forward.append(part / lower[i, i])
    back = [None] * ITERS
    for i in reversed(range(ITERS)):
        part = forward[i]
        for j in range(i + 1, ITERS):
            part = part - lower[j, i] * back[j]
        back[i] = part / lower[i, i]
    coef = []
    for m in range(ITERS):
        total = zero
        for j in range(m, ITERS):
            total = total + back[j] * basis[j][m]
        coef.append(total)
    lane = lax.broadcasted_iota(jnp.int32, (8, LANES), 1)
    dist = pltpu.roll(line, LANES - DIST, 1)
    dot = zero
    for m in range(ITERS):
        dot = dot + coef[m] * pltpu.roll(line, LANES - CROSS - KNOWN * m, 1)
    mean = dist / cells + EPS
    weight = 1.0 / mean + DEFLATE
    terms = jnp.where(lane < KNOWN, 2.0 * dot / (cells * mean * mean * weight), 0.0)
    total = jnp.sum(terms, axis=1, keepdims=True)
    tau = 1.0 / (1.0 + jnp.abs(jnp.broadcast_to(total, (8, LANES))))
    return [tau * a for a in coef]


def update(u_ref, w_refs, coef, dst, lo, hi):
    ncol = u_ref.shape[2] // LANES

    def body(x, carry):
        for t in range(u_ref.shape[1] // 8):
            for c in range(ncol):
                rows, cols = tile(t, c)
                value = u_ref[x, rows, cols]
                for a, w in zip(coef, w_refs):
                    value = value + a * w[x, rows, cols]
                dst[x, rows, cols] = value
        return carry

    lax.fori_loop(lo, hi, body, 0)


def first_kernel(mid_ref, lo_ref, hi_ref, known_hbm, u_ref, w0, w1, w2, sums_ref, known_ref, sems):
    inner = mid_ref.shape[0]
    copies = [
        pltpu.make_async_copy(lo_ref, u_ref.at[0:HX], sems.at[0]),
        pltpu.make_async_copy(mid_ref, u_ref.at[HX:HX + inner], sems.at[1]),
        pltpu.make_async_copy(hi_ref, u_ref.at[HX + inner:HX + inner + HX], sems.at[2]),
        pltpu.make_async_copy(known_hbm, known_ref, sems.at[3]),
    ]
    for copy in copies:
        copy.start()
    for copy in copies:
        copy.wait()
    planes = u_ref.shape[0]
    krylov(u_ref, (w0, w1, w2), None, 1, planes - 1, known_ref, sums_ref)


def second_kernel(cells, recv_ref, u_ref, a0, a1, a2, known_ref, v_ref, w0, w1, w2, sums_ref):
    coef = coefficients(recv_ref, cells)
    planes = u_ref.shape[0]
    update(u_ref, (a0, a1, a2), coef, v_ref, 3, planes - 3)
    krylov(v_ref, (w0, w1, w2), None, 4, planes - 4, known_ref, sums_ref)


def third_kernel(cells, recv_ref, u_ref, a0, a1, a2, out_ref, res_ref, v_ref):
    coef = coefficients(recv_ref, cells)
    planes = u_ref.shape[0]
    ncol = u_ref.shape[2] // LANES
    update(u_ref, (a0, a1, a2), coef, v_ref, HX - 1, planes - HX + 1)
    own = list(range(HY // 8, u_ref.shape[1] // 8 - HY // 8))

    def body(x, carry):
        for (t, c), (v, total) in plane_sums(v_ref, x, own, ncol).items():
            cols = slice(LANES * c, LANES * c + LANES)
            rows = slice(8 * t - HY, 8 * t - HY + 8)
            out_ref[x - HX, rows, cols] = v
            res_ref[x - HX, rows, cols] = 0.5 * total - v * (2.0 + v * v)
        return carry

    lax.fori_loop(HX, planes - HX, body, 0)


def total_over_devices(rows):
    count = rows.shape[0]
    rows = rows.reshape(count, 1, LANES)
    return lax.all_to_all(rows, AXES, 0, 0).reshape(count, LANES)


def shift(part, axis, step):
    count = lax.axis_size(axis)
    if step > 0:
        pairs = [(i, i + 1) for i in range(count - 1)]
    else:
        pairs = [(i + 1, i) for i in range(count - 1)]
    return lax.ppermute(part, axis, pairs)


def local(start_field, known):
    bx, by, bz = start_field.shape
    devices = lax.axis_size("px") * lax.axis_size("py")
    cells = float(bx * by * bz * devices)
    vmem = pl.BlockSpec(memory_space=pltpu.VMEM)
    hbm = pl.BlockSpec(memory_space=pl.ANY)
    params = pltpu.CompilerParams(vmem_limit_bytes=48 * 2**20)
    mid = jnp.concatenate(
        [shift(start_field[:, by - HY:], "py", 1), start_field, shift(start_field[:, :HY], "py", -1)], axis=1
    )
    lo = shift(mid[bx - HX:], "px", 1)
    hi = shift(mid[:HX], "px", -1)
    whole = jax.ShapeDtypeStruct((bx + 2 * HX, by + 2 * HY, bz), F32)
    sums = jax.ShapeDtypeStruct((devices, LANES), F32)
    own = jax.ShapeDtypeStruct((bx, by, bz), F32)
    u, a0, a1, a2, sent = pl.pallas_call(
        first_kernel,
        out_shape=(whole,) * 4 + (sums,),
        in_specs=[hbm] * 4,
        out_specs=(vmem,) * 5,
        scratch_shapes=[pltpu.VMEM(known.shape, F32), pltpu.SemaphoreType.DMA((4,))],
        compiler_params=params,
        name="first_step",
    )(mid, lo, hi, known)
    recv = total_over_devices(sent)
    v, b0, b1, b2, sent = pl.pallas_call(
        lambda *refs: second_kernel(cells, *refs),
        out_shape=(whole,) * 4 + (sums,),
        in_specs=[vmem] * 6,
        out_specs=(vmem,) * 5,
        compiler_params=params,
        name="second_step",
    )(recv, u, a0, a1, a2, known)
    recv = total_over_devices(sent)
    field, residual = pl.pallas_call(
        lambda *refs: third_kernel(cells, *refs),
        out_shape=(own, own),
        in_specs=[vmem] * 5,
        out_specs=(vmem, vmem),
        scratch_shapes=[pltpu.VMEM(whole.shape, F32)],
        compiler_params=params,
        name="finish",
    )(recv, v, b0, b1, b2)
    return field, residual


def solution(mesh):
    placed = (P("px", "py", None), P(None, "px", "py", None))
    return jax.shard_map(
        local,
        mesh=mesh,
        in_specs=placed,
        out_specs=(P("px", "py", None), P("px", "py", None)),
        check_vma=False,
    )
```

```python
import jax
import jax.numpy as jnp
from jax import lax
from jax.experimental import pallas as pl
from jax.experimental.pallas import tpu as pltpu
from jax.sharding import PartitionSpec as P

EPS = 1e-06
DEFLATE = 4.0
ITERS = 3
KNOWN = 8
AXES = ("px", "py")
HX = 7
HY = 8
LANES = 128
F32 = jnp.float32

DIST, CROSS = 8, 16


def iotas():
    row = lax.broadcasted_iota(jnp.int32, (8, LANES), 0)
    lane = lax.broadcasted_iota(jnp.int32, (8, LANES), 1)
    return row, lane


def plane_sums(ref, x, tiles, ncol):
    row, lane = iotas()
    top = ref.shape[1] // 8
    zero = jnp.zeros((8, LANES), F32)
    need = range(max(tiles[0] - 1, 0), min(tiles[-1] + 2, top))
    v = {(t, c): ref[x, 8 * t:8 * t + 8, LANES * c:LANES * c + LANES] for t in need for c in range(ncol)}
    up = {(t, c): pltpu.roll(v[t, c], 1, 0) for t in need if t <= tiles[-1] for c in range(ncol)}
    down = {(t, c): pltpu.roll(v[t, c], 7, 0) for t in need if t >= tiles[0] for c in range(ncol)}
    out = {}
    for t in tiles:
        before = jnp.where(lane == 0, zero, pltpu.roll(v[t, ncol - 1], 1, 1))
        after = jnp.where(lane == LANES - 1, zero, pltpu.roll(v[t, 0], LANES - 1, 1))
        for c in range(ncol):
            rows, cols = tile(t, c)
            a = up[t, c] if t == 0 else jnp.where(row == 0, up[t - 1, c], up[t, c])
            b = down[t, c] if t == top - 1 else jnp.where(row == 7, down[t + 1, c], down[t, c])
            l = v[t, c - 1] if c else before
            r = v[t, c + 1] if c < ncol - 1 else after
            total = (ref[x - 1, rows, cols] + ref[x + 1, rows, cols]) + (a + b) + (l + r)
            out[t, c] = (v[t, c], total)
    return out


def interleave(width, back):
    ncol = width // LANES
    dim_z, dim_p = (1, 0) if back else (0, 1)
    z = lax.broadcasted_iota(jnp.int32, (width, width), dim_z)
    p = lax.broadcasted_iota(jnp.int32, (width, width), dim_p)
    hit = z == (p % LANES) * ncol + p // LANES
    return jnp.where(hit, 1.0, 0.0).astype(jnp.bfloat16)


def move(value, matrix):
    total = None
    for _ in range(3):
        part = value.astype(jnp.bfloat16)
        value = value - part.astype(F32)
        piece = jnp.dot(part, matrix, preferred_element_type=F32)
        total = piece if total is None else total + piece
    return total


def tile(t, c):
    return slice(8 * t, 8 * t + 8), slice(LANES * c, LANES * c + LANES)


def edges():
    ix, iy = lax.axis_index("px"), lax.axis_index("py")
    nx, ny = lax.axis_size("px"), lax.axis_size("py")
    flag = lambda cond: jnp.where(cond, 0.0, 1.0).astype(F32)
    return flag(ix == 0), flag(ix == nx - 1), flag(iy == 0), flag(iy == ny - 1)


def krylov(u_ref, w_refs, lo, hi, known_ref, sums_ref):
    ncol = u_ref.shape[2] // LANES
    planes = u_ref.shape[0]
    top = u_ref.shape[1] // 8
    x_lo, x_hi, y_lo, y_hi = edges()
    first, last = HX, planes - HX

    def mask(x):
        m = jnp.where(x < first, x_lo, jnp.where(x >= last, x_hi, 1.0))
        return m

    def stage(k):
        src = u_ref if k == 0 else w_refs[k - 1]
        dst = w_refs[k]

        def body(x, carry):
            m = mask(x)
            sums = plane_sums(src, x, list(range(top)), ncol)
            for (t, c), (v, total) in sums.items():
                rows, cols = tile(t, c)
                if k == 0:
                    value = total - v * (4.0 + 2.0 * (v * v))
                else:
                    u = u_ref[x, rows, cols]
                    value = total + (2.0 - 6.0 * (u * u)) * v
                if t == 0:
                    value = value * (m * y_lo)
                elif t == top - 1:
                    value = value * (m * y_hi)
                else:
                    value = value * m
                dst[x, rows, cols] = value
            return carry

        lax.fori_loop(lo + k, hi - k, body, 0)

    for k in range(ITERS):
        stage(k)
    own = list(range(HY // 8, top - HY // 8))
    zero = jnp.zeros((8, LANES), F32)

    def moments(x, acc):
        acc = list(acc)
        sums = plane_sums(w_refs[2], x, own, ncol)
        for (t, c), (w2, total) in sums.items():
            rows, cols = tile(t, c)
            u = u_ref[x, rows, cols]
            w3 = total + (2.0 - 6.0 * (u * u)) * w2
            w0 = w_refs[0][x, rows, cols]
            w1 = w_refs[1][x, rows, cols]
            pairs = ((w0, w0), (w0, w1), (w1, w1), (w1, w2), (w2, w2), (w2, w3), (w3, w3))
            for n, (p, q) in enumerate(pairs):
                acc[n] = acc[n] + p * q
        return tuple(acc)

    acc = lax.fori_loop(first, last, moments, (zero,) * 7)

    def cross(x, acc):
        acc = list(acc)
        for t in own:
            for c in range(ncol):
                rows, cols = tile(t, c)
                u = u_ref[x, rows, cols]
                ws = [w_refs[m][x, rows, cols] for m in range(ITERS)]
                for i in range(KNOWN):
                    k = known_ref[i, x - first, slice(8 * t - HY, 8 * t - HY + 8), cols]
                    d = u - k
                    acc[i] = acc[i] + d * d
                    for m in range(ITERS):
                        acc[KNOWN * (m + 1) + i] = acc[KNOWN * (m + 1) + i] + d * ws[m]
        return tuple(acc)

    more = lax.fori_loop(first, last, cross, (zero,) * (KNOWN * (ITERS + 1)))
    parts = [jnp.sum(a, axis=0, keepdims=True) for a in (*acc, zero, *more)]
    block = jnp.concatenate(parts, axis=0)
    totals = jnp.sum(block, axis=1, keepdims=True)
    shape = block.shape
    hit = lax.broadcasted_iota(jnp.int32, shape, 0) == lax.broadcasted_iota(jnp.int32, shape, 1)
    line = jnp.sum(jnp.where(hit, totals, 0.0), axis=0, keepdims=True)
    sums_ref[...] = jnp.broadcast_to(line, sums_ref.shape)


def coefficients(recv_ref, cells):
    line = jnp.sum(recv_ref[...], axis=0, keepdims=True)
    line = jnp.broadcast_to(line, (8, LANES))
    mu = [jnp.broadcast_to(line[:, n:n + 1], (8, LANES)) for n in range(7)]
    zero = jnp.zeros((8, LANES), F32)

    def inner(p, q):
        total = None
        for i, a in enumerate(p):
            if a is None:
                continue
            part = None
            for j, b in enumerate(q):
                if b is None:
                    continue
                term = b * mu[i + j]
                part = term if part is None else part + term
            part = a * part
            total = part if total is None else total + part
        return total

    beta = jnp.sqrt(0.25 * mu[0] + EPS)
    basis = [[-0.5 / beta]]
    hess = {}
    for k in range(ITERS):
        vec = basis[k]
        image = [None] * (k + 2)
        for i in range(k + 2):
            a = 0.5 * vec[i - 1] if i > 0 else None
            b = -3.0 * vec[i] if i <= k else None
            image[i] = b if a is None else (a if b is None else a + b)
        for j in range(k + 1):
            hess[j, k] = inner(basis[j], image)
        rest = list(image)
        for j in range(k + 1):
            for i in range(len(basis[j])):
                rest[i] = rest[i] - hess[j, k] * basis[j][i]
        square = jnp.maximum(inner(rest, rest), 0.0)
        hess[k + 1, k] = jnp.sqrt(square + EPS)
        if k < ITERS - 1:
            scale = 1.0 / hess[k + 1, k]
            basis.append([a * scale for a in rest])

    def normal(i, j):
        total = None
        for r in range(ITERS + 1):
            if (r, i) in hess and (r, j) in hess:
                term = hess[r, i] * hess[r, j]
                total = term if total is None else total + term
        return total

    lower = {}
    for j in range(ITERS):
        diag = normal(j, j)
        for r in range(j):
            diag = diag - lower[j, r] * lower[j, r]
        lower[j, j] = jnp.sqrt(diag)
        for i in range(j + 1, ITERS):
            off = normal(i, j)
            for r in range(j):
                off = off - lower[i, r] * lower[j, r]
            lower[i, j] = off / lower[j, j]
    forward = []
    for i in range(ITERS):
        part = beta * hess[0, i]
        for j in range(i):
            part = part - lower[i, j] * forward[j]
        forward.append(part / lower[i, i])
    back = [None] * ITERS
    for i in reversed(range(ITERS)):
        part = forward[i]
        for j in range(i + 1, ITERS):
            part = part - lower[j, i] * back[j]
        back[i] = part / lower[i, i]
    coef = []
    for m in range(ITERS):
        total = zero
        for j in range(m, ITERS):
            total = total + back[j] * basis[j][m]
        coef.append(total)
    lane = lax.broadcasted_iota(jnp.int32, (8, LANES), 1)
    dist = pltpu.roll(line, LANES - DIST, 1)
    dot = zero
    for m in range(ITERS):
        dot = dot + coef[m] * pltpu.roll(line, LANES - CROSS - KNOWN * m, 1)
    mean = dist / cells + EPS
    weight = 1.0 / mean + DEFLATE
    terms = jnp.where(lane < KNOWN, 2.0 * dot / (cells * mean * mean * weight), 0.0)
    total = jnp.sum(terms, axis=1, keepdims=True)
    tau = 1.0 / (1.0 + jnp.abs(jnp.broadcast_to(total, (8, LANES))))
    return [tau * a for a in coef]


def update(u_ref, w_refs, coef, dst, lo, hi):
    ncol = u_ref.shape[2] // LANES

    def body(x, carry):
        for t in range(u_ref.shape[1] // 8):
            for c in range(ncol):
                rows, cols = tile(t, c)
                value = u_ref[x, rows, cols]
                for a, w in zip(coef, w_refs):
                    value = value + a * w[x, rows, cols]
                dst[x, rows, cols] = value
        return carry

    lax.fori_loop(lo, hi, body, 0)


def parity(axis):
    return lax.axis_index(axis) % 2


def spread_kernel(field_hbm, out_ref, first_ref, second_ref, field_ref, sem):
    copy = pltpu.make_async_copy(field_hbm, field_ref, sem)
    copy.start()
    bx, by, bz = out_ref.shape
    matrix = interleave(bz, False)
    copy.wait()
    out_ref[...] = move(field_ref[...].reshape(bx * by, bz), matrix).reshape(bx, by, bz)
    odd = parity("px")
    first_ref[...] = out_ref[pl.ds(1 - odd, HX)]
    second_ref[...] = out_ref[pl.ds(odd, HX)]


def known_kernel(known_ref, out_ref, back_ref):
    shape = known_ref.shape
    bz = shape[-1]
    matrix = interleave(bz, False)
    for i in range(shape[0]):
        part = move(known_ref[i].reshape(-1, bz), matrix)
        out_ref[i] = part.reshape(shape[1:])
    back_ref[...] = interleave(bz, True)


def join_kernel(own_ref, first_ref, second_ref, mid_ref, up_ref, down_ref):
    bx, by, bz = own_ref.shape
    odd = parity("px")
    mid_ref[pl.ds((1 - odd) * (HX + bx), HX)] = first_ref[...]
    mid_ref[pl.ds(odd * (HX + bx), HX)] = second_ref[...]
    mid_ref[HX:HX + bx] = own_ref[...]
    odd = parity("py")
    count = up_ref.shape[0]
    high = pl.multiple_of((1 - odd) * (by - HY), HY)
    low = pl.multiple_of(odd * (by - HY), HY)
    up_ref[...] = mid_ref[1:1 + count, pl.ds(high, HY)]
    down_ref[...] = mid_ref[1:1 + count, pl.ds(low, HY)]


def first_kernel(mid_ref, up_ref, down_ref, known_ref, u_ref, w0, w1, w2, sums_ref):
    planes, rows, bz = u_ref.shape
    by = rows - 2 * HY
    count = up_ref.shape[0]
    odd = parity("py")
    edge = jnp.zeros((1, HY, bz), F32)
    for x in (0, planes - 1):
        for y in (0, HY + by):
            u_ref[x:x + 1, y:y + HY] = edge
    u_ref[:, HY:HY + by] = mid_ref[...]
    high = pl.multiple_of((1 - odd) * (HY + by), HY)
    low = pl.multiple_of(odd * (HY + by), HY)
    u_ref[1:1 + count, pl.ds(high, HY)] = up_ref[...]
    u_ref[1:1 + count, pl.ds(low, HY)] = down_ref[...]
    krylov(u_ref, (w0, w1, w2), 1, planes - 1, known_ref, sums_ref)


def second_kernel(cells, recv_ref, u_ref, a0, a1, a2, known_ref, v_ref, w0, w1, w2, sums_ref):
    coef = coefficients(recv_ref, cells)
    planes = u_ref.shape[0]
    update(u_ref, (a0, a1, a2), coef, v_ref, 3, planes - 3)
    krylov(v_ref, (w0, w1, w2), 4, planes - 4, known_ref, sums_ref)


def third_kernel(cells, recv_ref, u_ref, a0, a1, a2, back_ref, out_ref, res_ref, v_ref, f_ref):
    coef = coefficients(recv_ref, cells)
    planes = u_ref.shape[0]
    ncol = u_ref.shape[2] // LANES
    update(u_ref, (a0, a1, a2), coef, v_ref, HX - 1, planes - HX + 1)
    own = list(range(HY // 8, u_ref.shape[1] // 8 - HY // 8))

    def body(x, carry):
        for (t, c), (v, total) in plane_sums(v_ref, x, own, ncol).items():
            cols = slice(LANES * c, LANES * c + LANES)
            rows = slice(8 * t - HY, 8 * t - HY + 8)
            f_ref[x - HX, rows, cols] = 0.5 * total - v * (2.0 + v * v)
        return carry

    lax.fori_loop(HX, planes - HX, body, 0)
    shape = out_ref.shape
    back = back_ref[...]
    mine = v_ref[HX:HX + shape[0], HY:HY + shape[1]]
    out_ref[...] = move(mine.reshape(-1, shape[2]), back).reshape(shape)
    res_ref[...] = move(f_ref[...].reshape(-1, shape[2]), back).reshape(shape)


def total_over_devices(rows):
    count = rows.shape[0]
    rows = rows.reshape(count, 1, LANES)
    return lax.all_to_all(rows, AXES, 0, 0).reshape(count, LANES)


def swap(part, axis, first):
    pairs = []
    for i in range(first, lax.axis_size(axis) - 1, 2):
        pairs += [(i, i + 1), (i + 1, i)]
    return lax.ppermute(part, axis, pairs)


def local(start_field, known):
    bx, by, bz = start_field.shape
    devices = lax.axis_size("px") * lax.axis_size("py")
    cells = float(bx * by * bz * devices)
    vmem = pl.BlockSpec(memory_space=pltpu.VMEM)
    hbm = pl.BlockSpec(memory_space=pl.ANY)
    params = pltpu.CompilerParams(vmem_limit_bytes=24 * 2**20)
    shape = lambda *dims: jax.ShapeDtypeStruct(dims, F32)

    def call(body, name, outs, *args, specs=None, scratch=()):
        return pl.pallas_call(
            body,
            out_shape=outs,
            in_specs=[vmem] * len(args) if specs is None else specs,
            out_specs=tuple(vmem for _ in outs),
            scratch_shapes=scratch,
            compiler_params=params,
            name=name,
        )(*args)

    planes, rows = bx + 2 * HX, by + 2 * HY
    side = shape(HX, by, bz)
    mine, first, second = call(
        spread_kernel,
        "spread",
        (shape(bx, by, bz), side, side),
        start_field,
        specs=[hbm],
        scratch=[pltpu.VMEM((bx, by, bz), F32), pltpu.SemaphoreType.DMA],
    )
    first, second = swap(first, "px", 0), swap(second, "px", 1)
    known, back = pl.pallas_call(
        known_kernel,
        out_shape=(jax.ShapeDtypeStruct(known.shape, F32), jax.ShapeDtypeStruct((bz, bz), jnp.bfloat16)),
        in_specs=[vmem],
        out_specs=(vmem, vmem),
        compiler_params=params,
        name="known_spread",
    )(known)
    strip = shape(planes - 2, HY, bz)
    mid, up, down = call(join_kernel, "join", (shape(planes, by, bz), strip, strip), mine, first, second)
    up, down = swap(up, "py", 0), swap(down, "py", 1)
    whole = shape(planes, rows, bz)
    sums = shape(devices, LANES)
    own = shape(bx, by, bz)
    u, a0, a1, a2, sent = call(first_kernel, "first_step", (whole,) * 4 + (sums,), mid, up, down, known)
    recv = total_over_devices(sent)
    body = lambda *refs: second_kernel(cells, *refs)
    v, b0, b1, b2, sent = call(body, "second_step", (whole,) * 4 + (sums,), recv, u, a0, a1, a2, known)
    recv = total_over_devices(sent)
    body = lambda *refs: third_kernel(cells, *refs)
    scratch = [pltpu.VMEM(whole.shape, F32), pltpu.VMEM(own.shape, F32)]
    field, residual = call(body, "finish", (own, own), recv, v, b0, b1, b2, back, scratch=scratch)
    return field, residual


def solution(mesh):
    placed = (P("px", "py", None), P(None, "px", "py", None))
    return jax.shard_map(
        local,
        mesh=mesh,
        in_specs=placed,
        out_specs=(P("px", "py", None), P("px", "py", None)),
        check_vma=False,
    )
```

```python
import jax
import jax.numpy as jnp
from jax import lax
from jax.experimental import pallas as pl
from jax.experimental.pallas import tpu as pltpu
from jax.sharding import PartitionSpec as P

EPS = 1e-06
DEFLATE = 4.0
ITERS = 3
KNOWN = 8
AXES = ("px", "py")
HX = 7
HY = 8
LANES = 128
F32 = jnp.float32

DIST, CROSS = 8, 16


def iotas():
    row = lax.broadcasted_iota(jnp.int32, (8, LANES), 0)
    lane = lax.broadcasted_iota(jnp.int32, (8, LANES), 1)
    return row, lane


def plane_sums(ref, x, tiles):
    row, lane = iotas()
    top, ncol = ref.shape[1] // 8, ref.shape[2] // LANES
    zero = jnp.zeros((8, LANES), F32)
    need = range(max(tiles[0] - 1, 0), min(tiles[-1] + 2, top))
    v = {(t, c): ref[(x, *tile(t, c))] for t in need for c in range(ncol)}
    up = {(t, c): pltpu.roll(v[t, c], 1, 0) for t in need if t <= tiles[-1] for c in range(ncol)}
    down = {(t, c): pltpu.roll(v[t, c], 7, 0) for t in need if t >= tiles[0] for c in range(ncol)}
    for t in tiles:
        left = [zero] + [pltpu.roll(v[t, c], 1, 1) for c in range(ncol)]
        right = [pltpu.roll(v[t, c], LANES - 1, 1) for c in range(ncol)] + [zero]
        for c in range(ncol):
            a = up[t, c] if t == 0 else jnp.where(row == 0, up[t - 1, c], up[t, c])
            b = down[t, c] if t == top - 1 else jnp.where(row == 7, down[t + 1, c], down[t, c])
            l = jnp.where(lane == 0, left[c], left[c + 1])
            r = jnp.where(lane == LANES - 1, right[c + 1], right[c])
            where = tile(t, c)
            total = (ref[(x - 1, *where)] + ref[(x + 1, *where)]) + (a + b) + (l + r)
            yield t, c, v[t, c], total


def tile(t, c):
    return slice(8 * t, 8 * t + 8), slice(LANES * c, LANES * c + LANES)


def edges():
    ix, iy = lax.axis_index("px"), lax.axis_index("py")
    nx, ny = lax.axis_size("px"), lax.axis_size("py")
    flag = lambda cond: jnp.where(cond, 0.0, 1.0).astype(F32)
    return flag(ix == 0), flag(ix == nx - 1), flag(iy == 0), flag(iy == ny - 1)


def krylov(u_ref, w_refs, lo, hi, known_ref, sums_ref):
    planes, top, ncol = u_ref.shape[0], u_ref.shape[1] // 8, u_ref.shape[2] // LANES
    x_lo, x_hi, y_lo, y_hi = edges()
    first, last = HX, planes - HX

    def mask(x, t):
        along = x_lo if x < first else x_hi if x >= last else None
        across = y_lo if t == 0 else y_hi if t == top - 1 else None
        if along is None or across is None:
            return across if along is None else along
        return along * across

    for k in range(ITERS):
        src, dst = u_ref if k == 0 else w_refs[k - 1], w_refs[k]
        for x in range(lo + k, hi - k):
            for t, c, v, total in plane_sums(src, x, range(top)):
                if k == 0:
                    value = total - v * (4.0 + 2.0 * (v * v))
                else:
                    u = u_ref[(x, *tile(t, c))]
                    value = total + (2.0 - 6.0 * (u * u)) * v
                m = mask(x, t)
                dst[(x, *tile(t, c))] = value if m is None else value * m
    own = range(HY // 8, top - HY // 8)
    zero = jnp.zeros((8, LANES), F32)
    mus = [zero] * 8
    more = [zero] * (KNOWN * (ITERS + 1))
    for x in range(first, last):
        for t, c, w2, total in plane_sums(w_refs[2], x, own):
            u, w0, w1 = (ref[(x, *tile(t, c))] for ref in (u_ref, w_refs[0], w_refs[1]))
            w3 = total + (2.0 - 6.0 * (u * u)) * w2
            pairs = ((w0, w0), (w0, w1), (w1, w1), (w1, w2), (w2, w2), (w2, w3), (w3, w3))
            for n, (p, q) in enumerate(pairs):
                mus[n] = mus[n] + p * q
    for x in range(first, last):
        for t in own:
            for c in range(ncol):
                u, *ws = (ref[(x, *tile(t, c))] for ref in (u_ref, *w_refs))
                for i in range(KNOWN):
                    d = u - known_ref[(i, x - first, *tile(t - HY // 8, c))]
                    more[i] = more[i] + d * d
                    for m in range(ITERS):
                        n = KNOWN * (m + 1) + i
                        more[n] = more[n] + d * ws[m]
    block = jnp.concatenate([jnp.sum(a, axis=0, keepdims=True) for a in (*mus, *more)], axis=0)
    totals = jnp.sum(block, axis=1, keepdims=True)
    hit = lax.broadcasted_iota(jnp.int32, block.shape, 0) == lax.broadcasted_iota(jnp.int32, block.shape, 1)
    line = jnp.sum(jnp.where(hit, totals, 0.0), axis=0, keepdims=True)
    sums_ref[...] = jnp.broadcast_to(line, sums_ref.shape)


def coefficients(recv_ref, cells):
    line = jnp.sum(recv_ref[...], axis=0, keepdims=True)
    line = jnp.broadcast_to(line, (8, LANES))
    mu = [jnp.broadcast_to(line[:, n:n + 1], (8, LANES)) for n in range(7)]
    zero = jnp.zeros((8, LANES), F32)

    def inner(p, q):
        total = None
        for i, a in enumerate(p):
            if a is None:
                continue
            part = None
            for j, b in enumerate(q):
                if b is None:
                    continue
                term = b * mu[i + j]
                part = term if part is None else part + term
            part = a * part
            total = part if total is None else total + part
        return total

    beta = jnp.sqrt(0.25 * mu[0] + EPS)
    basis = [[-0.5 / beta]]
    hess = {}
    for k in range(ITERS):
        vec = basis[k]
        image = [None] * (k + 2)
        for i in range(k + 2):
            a = 0.5 * vec[i - 1] if i > 0 else None
            b = -3.0 * vec[i] if i <= k else None
            image[i] = b if a is None else (a if b is None else a + b)
        for j in range(k + 1):
            hess[j, k] = inner(basis[j], image)
        rest = list(image)
        for j in range(k + 1):
            for i in range(len(basis[j])):
                rest[i] = rest[i] - hess[j, k] * basis[j][i]
        square = jnp.maximum(inner(rest, rest), 0.0)
        hess[k + 1, k] = jnp.sqrt(square + EPS)
        if k < ITERS - 1:
            scale = 1.0 / hess[k + 1, k]
            basis.append([a * scale for a in rest])

    def normal(i, j):
        total = None
        for r in range(ITERS + 1):
            if (r, i) in hess and (r, j) in hess:
                term = hess[r, i] * hess[r, j]
                total = term if total is None else total + term
        return total

    lower = {}
    for j in range(ITERS):
        diag = normal(j, j)
        for r in range(j):
            diag = diag - lower[j, r] * lower[j, r]
        lower[j, j] = jnp.sqrt(diag)
        for i in range(j + 1, ITERS):
            off = normal(i, j)
            for r in range(j):
                off = off - lower[i, r] * lower[j, r]
            lower[i, j] = off / lower[j, j]
    forward = []
    for i in range(ITERS):
        part = beta * hess[0, i]
        for j in range(i):
            part = part - lower[i, j] * forward[j]
        forward.append(part / lower[i, i])
    back = [None] * ITERS
    for i in reversed(range(ITERS)):
        part = forward[i]
        for j in range(i + 1, ITERS):
            part = part - lower[j, i] * back[j]
        back[i] = part / lower[i, i]
    coef = []
    for m in range(ITERS):
        total = zero
        for j in range(m, ITERS):
            total = total + back[j] * basis[j][m]
        coef.append(total)
    lane = lax.broadcasted_iota(jnp.int32, (8, LANES), 1)
    dist = pltpu.roll(line, LANES - DIST, 1)
    dot = zero
    for m in range(ITERS):
        dot = dot + coef[m] * pltpu.roll(line, LANES - CROSS - KNOWN * m, 1)
    mean = dist / cells + EPS
    weight = 1.0 / mean + DEFLATE
    terms = jnp.where(lane < KNOWN, 2.0 * dot / (cells * mean * mean * weight), 0.0)
    total = jnp.sum(terms, axis=1, keepdims=True)
    tau = 1.0 / (1.0 + jnp.abs(jnp.broadcast_to(total, (8, LANES))))
    return [tau * a for a in coef]


def update(u_ref, w_refs, coef, dst, lo, hi):
    top, ncol = u_ref.shape[1] // 8, u_ref.shape[2] // LANES
    for x in range(lo, hi):
        for t in range(top):
            for c in range(ncol):
                where = (x, *tile(t, c))
                value = u_ref[where]
                for a, w in zip(coef, w_refs):
                    value = value + a * w[where]
                dst[where] = value


def parity(axis):
    return lax.axis_index(axis) % 2


def load_kernel(field_hbm, known_hbm, field_ref, known_ref, sems):
    pairs = ((field_hbm, field_ref), (known_hbm, known_ref))
    copies = [pltpu.make_async_copy(a, b, sems.at[n]) for n, (a, b) in enumerate(pairs)]
    for copy in copies:
        copy.start()
    for copy in copies:
        copy.wait()


def join_kernel(own_ref, first_ref, second_ref, mid_ref, up_ref, down_ref):
    bx, by, bz = own_ref.shape
    odd = parity("px")
    mid_ref[pl.ds((1 - odd) * (HX + bx), HX)] = first_ref[pl.ds(odd * (bx - HX), HX)]
    mid_ref[pl.ds(odd * (HX + bx), HX)] = second_ref[pl.ds((1 - odd) * (bx - HX), HX)]
    mid_ref[HX:HX + bx] = own_ref[...]
    odd = parity("py")
    count = up_ref.shape[0]
    high = pl.multiple_of((1 - odd) * (by - HY), HY)
    low = pl.multiple_of(odd * (by - HY), HY)
    up_ref[...] = mid_ref[1:1 + count, pl.ds(high, HY)]
    down_ref[...] = mid_ref[1:1 + count, pl.ds(low, HY)]


def first_kernel(mid_ref, up_ref, down_ref, known_ref, u_ref, w0, w1, w2, sums_ref):
    planes, rows, bz = u_ref.shape
    by = rows - 2 * HY
    count = up_ref.shape[0]
    odd = parity("py")
    edge = jnp.zeros((1, HY, bz), F32)
    for x in (0, planes - 1):
        for y in (0, HY + by):
            u_ref[x:x + 1, y:y + HY] = edge
    u_ref[:, HY:HY + by] = mid_ref[...]
    high = pl.multiple_of((1 - odd) * (HY + by), HY)
    low = pl.multiple_of(odd * (HY + by), HY)
    u_ref[1:1 + count, pl.ds(high, HY)] = up_ref[...]
    u_ref[1:1 + count, pl.ds(low, HY)] = down_ref[...]
    krylov(u_ref, (w0, w1, w2), 1, planes - 1, known_ref, sums_ref)


def second_kernel(cells, recv_ref, u_ref, a0, a1, a2, known_ref, v_ref, w0, w1, w2, sums_ref):
    coef = coefficients(recv_ref, cells)
    planes = u_ref.shape[0]
    update(u_ref, (a0, a1, a2), coef, v_ref, 3, planes - 3)
    krylov(v_ref, (w0, w1, w2), 4, planes - 4, known_ref, sums_ref)


def third_kernel(cells, recv_ref, u_ref, a0, a1, a2, out_ref, res_ref, v_ref):
    coef = coefficients(recv_ref, cells)
    planes, top = u_ref.shape[0], u_ref.shape[1] // 8
    update(u_ref, (a0, a1, a2), coef, v_ref, HX - 1, planes - HX + 1)
    for x in range(HX, planes - HX):
        for t, c, v, total in plane_sums(v_ref, x, range(HY // 8, top - HY // 8)):
            where = (x - HX, *tile(t - HY // 8, c))
            out_ref[where] = v
            res_ref[where] = 0.5 * total - v * (2.0 + v * v)


def total_over_devices(rows):
    count = rows.shape[0]
    rows = rows.reshape(count, 1, LANES)
    return lax.all_to_all(rows, AXES, 0, 0).reshape(count, LANES)


def swap(part, axis, first):
    pairs = []
    for i in range(first, lax.axis_size(axis) - 1, 2):
        pairs += [(i, i + 1), (i + 1, i)]
    return lax.ppermute(part, axis, pairs)


def local(start_field, known):
    bx, by, bz = start_field.shape
    devices = lax.axis_size("px") * lax.axis_size("py")
    cells = float(bx * by * bz * devices)
    vmem = pl.BlockSpec(memory_space=pltpu.VMEM)
    params = pltpu.CompilerParams(vmem_limit_bytes=24 * 2**20)
    shape = lambda *dims: jax.ShapeDtypeStruct(dims, F32)

    def call(body, name, outs, *args, scratch=(), space=pltpu.VMEM):
        return pl.pallas_call(
            body,
            out_shape=outs,
            in_specs=[pl.BlockSpec(memory_space=space)] * len(args),
            out_specs=tuple(vmem for _ in outs),
            scratch_shapes=scratch,
            compiler_params=params,
            name=name,
        )(*args)

    planes, rows = bx + 2 * HX, by + 2 * HY
    first, second = swap(start_field, "px", 0), swap(start_field, "px", 1)
    own = shape(bx, by, bz)
    sems = [pltpu.SemaphoreType.DMA((2,))]
    loaded = (own, shape(*known.shape))
    mine, known = call(load_kernel, "load", loaded, start_field, known, scratch=sems, space=pltpu.HBM)
    strip = shape(planes - 2, HY, bz)
    mid, up, down = call(join_kernel, "join", (shape(planes, by, bz), strip, strip), mine, first, second)
    up, down = swap(up, "py", 0), swap(down, "py", 1)
    whole = shape(planes, rows, bz)
    sums = shape(devices, LANES)
    u, a0, a1, a2, sent = call(first_kernel, "first_step", (whole,) * 4 + (sums,), mid, up, down, known)
    recv = total_over_devices(sent)
    body = lambda *refs: second_kernel(cells, *refs)
    v, b0, b1, b2, sent = call(body, "second_step", (whole,) * 4 + (sums,), recv, u, a0, a1, a2, known)
    recv = total_over_devices(sent)
    body = lambda *refs: third_kernel(cells, *refs)
    scratch = [pltpu.VMEM(whole.shape, F32)]
    field, residual = call(body, "finish", (own, own), recv, v, b0, b1, b2, scratch=scratch)
    return field, residual


def solution(mesh):
    placed = (P("px", "py", None), P(None, "px", "py", None))
    return jax.shard_map(
        local,
        mesh=mesh,
        in_specs=placed,
        out_specs=(P("px", "py", None), P("px", "py", None)),
        check_vma=False,
    )
```

```python
import jax
import jax.numpy as jnp
from jax import lax
from jax.experimental import pallas as pl
from jax.experimental.pallas import tpu as pltpu
from jax.sharding import PartitionSpec as P

EPS = 1e-06
DEFLATE = 4.0
ITERS = 3
KNOWN = 8
AXES = ("px", "py")
HX = 7
HY = 8
LANES = 128
F32 = jnp.float32

DIST, CROSS = 8, 16


def iotas():
    row = lax.broadcasted_iota(jnp.int32, (8, LANES), 0)
    lane = lax.broadcasted_iota(jnp.int32, (8, LANES), 1)
    return row, lane


def plane_sums(ref, x, tiles):
    row, lane = iotas()
    top, ncol = ref.shape[1] // 8, ref.shape[2] // LANES
    zero = jnp.zeros((8, LANES), F32)
    need = range(max(tiles[0] - 1, 0), min(tiles[-1] + 2, top))
    v = {(t, c): ref[(x, *tile(t, c))] for t in need for c in range(ncol)}
    up = {(t, c): pltpu.roll(v[t, c], 1, 0) for t in need if t <= tiles[-1] for c in range(ncol)}
    down = {(t, c): pltpu.roll(v[t, c], 7, 0) for t in need if t >= tiles[0] for c in range(ncol)}
    for t in tiles:
        left = [zero] + [pltpu.roll(v[t, c], 1, 1) for c in range(ncol)]
        right = [pltpu.roll(v[t, c], LANES - 1, 1) for c in range(ncol)] + [zero]
        for c in range(ncol):
            a = up[t, c] if t == 0 else jnp.where(row == 0, up[t - 1, c], up[t, c])
            b = down[t, c] if t == top - 1 else jnp.where(row == 7, down[t + 1, c], down[t, c])
            l = jnp.where(lane == 0, left[c], left[c + 1])
            r = jnp.where(lane == LANES - 1, right[c + 1], right[c])
            where = tile(t, c)
            total = (ref[(x - 1, *where)] + ref[(x + 1, *where)]) + (a + b) + (l + r)
            yield t, c, v[t, c], total


def tile(t, c):
    return slice(8 * t, 8 * t + 8), slice(LANES * c, LANES * c + LANES)


def edges():
    ix, iy = lax.axis_index("px"), lax.axis_index("py")
    nx, ny = lax.axis_size("px"), lax.axis_size("py")
    flag = lambda cond: jnp.where(cond, 0.0, 1.0).astype(F32)
    return flag(ix == 0), flag(ix == nx - 1), flag(iy == 0), flag(iy == ny - 1)


def krylov(u_ref, w_refs, lo, hi, known_ref, gap, sums_ref):
    planes, top, ncol = u_ref.shape[0], u_ref.shape[1] // 8, u_ref.shape[2] // LANES
    x_lo, x_hi, y_lo, y_hi = edges()
    first, last = HX, planes - HX

    def mask(x, t):
        along = x_lo if x < first else x_hi if x >= last else None
        across = y_lo if t == 0 else y_hi if t == top - 1 else None
        if along is None or across is None:
            return across if along is None else along
        return along * across

    for k in range(ITERS):
        src, dst = u_ref if k == 0 else w_refs[k - 1], w_refs[k]
        for x in range(lo + k, hi - k):
            for t, c, v, total in plane_sums(src, x, range(top)):
                if k == 0:
                    value = total - v * (4.0 + 2.0 * (v * v))
                else:
                    u = u_ref[(x, *tile(t, c))]
                    value = total + (2.0 - 6.0 * (u * u)) * v
                m = mask(x, t)
                dst[(x, *tile(t, c))] = value if m is None else value * m
    own = range(HY // 8, top - HY // 8)
    zero = jnp.zeros((8, LANES), F32)
    mus = [zero] * 8
    more = [zero] * (KNOWN * (ITERS + 1))
    if gap is not None:
        more[:KNOWN] = [gap[1][i] for i in range(KNOWN)]
    for x in range(first, last):
        for t, c, w2, total in plane_sums(w_refs[2], x, own):
            u, w0, w1 = (ref[(x, *tile(t, c))] for ref in (u_ref, w_refs[0], w_refs[1]))
            w3 = total + (2.0 - 6.0 * (u * u)) * w2
            pairs = ((w0, w0), (w0, w1), (w1, w1), (w1, w2), (w2, w2), (w2, w3), (w3, w3))
            for n, (p, q) in enumerate(pairs):
                mus[n] = mus[n] + p * q
    for x in range(first, last):
        for t in own:
            for c in range(ncol):
                u, *ws = (ref[(x, *tile(t, c))] for ref in (u_ref, *w_refs))
                for i in range(KNOWN):
                    where = (i, x - first, *tile(t - HY // 8, c))
                    if gap is None:
                        d = u - known_ref[where]
                        more[i] = more[i] + d * d
                    else:
                        d = gap[0][where]
                    for m in range(ITERS):
                        n = KNOWN * (m + 1) + i
                        more[n] = more[n] + d * ws[m]
    block = jnp.concatenate([jnp.sum(a, axis=0, keepdims=True) for a in (*mus, *more)], axis=0)
    totals = jnp.sum(block, axis=1, keepdims=True)
    hit = lax.broadcasted_iota(jnp.int32, block.shape, 0) == lax.broadcasted_iota(jnp.int32, block.shape, 1)
    line = jnp.sum(jnp.where(hit, totals, 0.0), axis=0, keepdims=True)
    sums_ref[...] = jnp.broadcast_to(line, sums_ref.shape)


def coefficients(recv_ref, cells):
    line = jnp.sum(recv_ref[...], axis=0, keepdims=True)
    line = jnp.broadcast_to(line, (8, LANES))
    mu = [jnp.broadcast_to(line[:, n:n + 1], (8, LANES)) for n in range(7)]
    zero = jnp.zeros((8, LANES), F32)

    def inner(p, q):
        total = None
        for i, a in enumerate(p):
            if a is None:
                continue
            part = None
            for j, b in enumerate(q):
                if b is None:
                    continue
                term = b * mu[i + j]
                part = term if part is None else part + term
            part = a * part
            total = part if total is None else total + part
        return total

    beta = jnp.sqrt(0.25 * mu[0] + EPS)
    basis = [[-0.5 / beta]]
    hess = {}
    for k in range(ITERS):
        vec = basis[k]
        image = [None] * (k + 2)
        for i in range(k + 2):
            a = 0.5 * vec[i - 1] if i > 0 else None
            b = -3.0 * vec[i] if i <= k else None
            image[i] = b if a is None else (a if b is None else a + b)
        for j in range(k + 1):
            hess[j, k] = inner(basis[j], image)
        rest = list(image)
        for j in range(k + 1):
            for i in range(len(basis[j])):
                rest[i] = rest[i] - hess[j, k] * basis[j][i]
        square = jnp.maximum(inner(rest, rest), 0.0)
        hess[k + 1, k] = jnp.sqrt(square + EPS)
        if k < ITERS - 1:
            scale = 1.0 / hess[k + 1, k]
            basis.append([a * scale for a in rest])

    def normal(i, j):
        total = None
        for r in range(ITERS + 1):
            if (r, i) in hess and (r, j) in hess:
                term = hess[r, i] * hess[r, j]
                total = term if total is None else total + term
        return total

    lower = {}
    for j in range(ITERS):
        diag = normal(j, j)
        for r in range(j):
            diag = diag - lower[j, r] * lower[j, r]
        lower[j, j] = jnp.sqrt(diag)
        for i in range(j + 1, ITERS):
            off = normal(i, j)
            for r in range(j):
                off = off - lower[i, r] * lower[j, r]
            lower[i, j] = off / lower[j, j]
    forward = []
    for i in range(ITERS):
        part = beta * hess[0, i]
        for j in range(i):
            part = part - lower[i, j] * forward[j]
        forward.append(part / lower[i, i])
    back = [None] * ITERS
    for i in reversed(range(ITERS)):
        part = forward[i]
        for j in range(i + 1, ITERS):
            part = part - lower[j, i] * back[j]
        back[i] = part / lower[i, i]
    coef = []
    for m in range(ITERS):
        total = zero
        for j in range(m, ITERS):
            total = total + back[j] * basis[j][m]
        coef.append(total)
    lane = lax.broadcasted_iota(jnp.int32, (8, LANES), 1)
    dist = pltpu.roll(line, LANES - DIST, 1)
    dot = zero
    for m in range(ITERS):
        dot = dot + coef[m] * pltpu.roll(line, LANES - CROSS - KNOWN * m, 1)
    mean = dist / cells + EPS
    weight = 1.0 / mean + DEFLATE
    terms = jnp.where(lane < KNOWN, 2.0 * dot / (cells * mean * mean * weight), 0.0)
    total = jnp.sum(terms, axis=1, keepdims=True)
    tau = 1.0 / (1.0 + jnp.abs(jnp.broadcast_to(total, (8, LANES))))
    return [tau * a for a in coef]


def update(u_ref, w_refs, coef, dst, lo, hi):
    top, ncol = u_ref.shape[1] // 8, u_ref.shape[2] // LANES
    for x in range(lo, hi):
        for t in range(top):
            for c in range(ncol):
                where = (x, *tile(t, c))
                value = u_ref[where]
                for a, w in zip(coef, w_refs):
                    value = value + a * w[where]
                dst[where] = value


def parity(axis):
    return lax.axis_index(axis) % 2


def edge_kernel(field_ref, rows_ref):
    by = field_ref.shape[1]
    start = pl.multiple_of(parity("py") * (by - HY), HY)
    rows_ref[...] = field_ref[:, pl.ds(start, HY)]


def gap_kernel(field_ref, known_ref, out_ref, gap_ref, dist_ref):
    count, bx, by, bz = known_ref.shape
    for i in range(count):
        total = None
        for x in range(bx):
            for t in range(by // 8):
                for c in range(bz // LANES):
                    where = tile(t, c)
                    k = known_ref[(i, x, *where)]
                    d = field_ref[(x, *where)] - k
                    out_ref[(i, x, *where)] = k
                    gap_ref[(i, x, *where)] = d
                    total = d * d if total is None else total + d * d
        dist_ref[i] = total


def strip_planes(planes):
    last = planes - 1
    full = (5, 6, last - 6, last - 5)
    pairs = ((1, 2), (3, 4), (last - 4, last - 3), (last - 2, last - 1))
    return full, pairs


def half_turn(value, flag):
    return jnp.where(flag, pltpu.roll(value, 4, 0), value)


def join_kernel(own_ref, first_ref, second_ref, rows_ref, u_ref, up_ref, strip_ref):
    bx, by, bz = own_ref.shape
    planes = u_ref.shape[0]
    mine = slice(HY, HY + by)
    odd = parity("px")
    u_ref[pl.ds((1 - odd) * (HX + bx), HX), mine] = first_ref[pl.ds(odd * (bx - HX), HX)]
    u_ref[pl.ds(odd * (HX + bx), HX), mine] = second_ref[pl.ds((1 - odd) * (bx - HX), HX)]
    u_ref[HX:HX + bx, mine] = own_ref[...]
    odd = parity("py")
    u_ref[HX:HX + bx, pl.ds(pl.multiple_of(odd * (HY + by), HY), HY)] = rows_ref[...]
    count = up_ref.shape[0]
    high = pl.multiple_of(HY + (1 - odd) * (by - HY), HY)
    low = pl.multiple_of(HY + odd * (by - HY), HY)
    up_ref[...] = u_ref[1:1 + count, pl.ds(high, HY)]
    row, _ = iotas()
    full, pairs = strip_planes(planes)
    for n, x in enumerate(full):
        strip_ref[n] = u_ref[x, pl.ds(low, HY)]
    for n, (x, y) in enumerate(pairs):
        for c in range(bz // LANES):
            cols = slice(LANES * c, LANES * c + LANES)
            a = half_turn(u_ref[x, pl.ds(low, HY), cols], odd == 1)
            b = half_turn(u_ref[y, pl.ds(low, HY), cols], odd == 0)
            strip_ref[len(full) + n, :, cols] = jnp.where(row < 4, a, b)


def first_kernel(mid_ref, up_ref, strip_ref, gap_ref, dist_ref, u_ref, w0, w1, w2, sums_ref):
    planes, rows, bz = u_ref.shape
    by = rows - 2 * HY
    count = up_ref.shape[0]
    odd = parity("py")
    edge = jnp.zeros((1, HY, bz), F32)
    for x in (0, planes - 1):
        for y in (0, HY + by):
            u_ref[x:x + 1, y:y + HY] = edge
    high = pl.multiple_of((1 - odd) * (HY + by), HY)
    low = pl.multiple_of(odd * (HY + by), HY)
    u_ref[1:1 + count, pl.ds(high, HY)] = up_ref[...]
    full, pairs = strip_planes(planes)
    for n, x in enumerate(full):
        u_ref[x, pl.ds(low, HY)] = strip_ref[n]
    for n, (x, y) in enumerate(pairs):
        for c in range(bz // LANES):
            cols = slice(LANES * c, LANES * c + LANES)
            both = strip_ref[len(full) + n, :, cols]
            u_ref[x, pl.ds(low, HY), cols] = half_turn(both, odd == 0)
            u_ref[y, pl.ds(low, HY), cols] = half_turn(both, odd == 1)
    krylov(u_ref, (w0, w1, w2), 1, planes - 1, None, (gap_ref, dist_ref), sums_ref)


def second_kernel(cells, recv_ref, u_ref, a0, a1, a2, known_ref, v_ref, w0, w1, w2, sums_ref):
    coef = coefficients(recv_ref, cells)
    planes = u_ref.shape[0]
    update(u_ref, (a0, a1, a2), coef, v_ref, 3, planes - 3)
    krylov(v_ref, (w0, w1, w2), 4, planes - 4, known_ref, None, sums_ref)


def third_kernel(cells, recv_ref, u_ref, a0, a1, a2, out_ref, res_ref, v_ref):
    coef = coefficients(recv_ref, cells)
    planes, top = u_ref.shape[0], u_ref.shape[1] // 8
    update(u_ref, (a0, a1, a2), coef, v_ref, HX - 1, planes - HX + 1)
    for x in range(HX, planes - HX):
        for t, c, v, total in plane_sums(v_ref, x, range(HY // 8, top - HY // 8)):
            where = (x - HX, *tile(t - HY // 8, c))
            out_ref[where] = v
            res_ref[where] = 0.5 * total - v * (2.0 + v * v)


def total_over_devices(rows):
    count = rows.shape[0]
    rows = rows.reshape(count, 1, LANES)
    return lax.all_to_all(rows, AXES, 0, 0).reshape(count, LANES)


def swap(part, axis, first):
    pairs = []
    for i in range(first, lax.axis_size(axis) - 1, 2):
        pairs += [(i, i + 1), (i + 1, i)]
    return lax.ppermute(part, axis, pairs)


def local(start_field, known):
    bx, by, bz = start_field.shape
    devices = lax.axis_size("px") * lax.axis_size("py")
    cells = float(bx * by * bz * devices)
    vmem = pl.BlockSpec(memory_space=pltpu.VMEM)
    params = pltpu.CompilerParams(vmem_limit_bytes=24 * 2**20)
    shape = lambda *dims: jax.ShapeDtypeStruct(dims, F32)

    def call(body, name, outs, *args, scratch=(), alias={}):
        return pl.pallas_call(
            body,
            out_shape=outs,
            in_specs=[vmem] * len(args),
            out_specs=tuple(vmem for _ in outs),
            scratch_shapes=scratch,
            input_output_aliases=alias,
            compiler_params=params,
            name=name,
        )(*args)

    planes, rows = bx + 2 * HX, by + 2 * HY
    own, whole = shape(bx, by, bz), shape(planes, rows, bz)
    sums = shape(devices, LANES)
    first, second = swap(start_field, "px", 0), swap(start_field, "px", 1)
    (edge,) = call(edge_kernel, "edge", (shape(bx, HY, bz),), start_field)
    edge = swap(edge, "py", 1)
    full, pairs = strip_planes(planes)
    parts = (whole, shape(planes - 2, HY, bz), shape(len(full) + len(pairs), HY, bz))
    u, up, strip = call(join_kernel, "join", parts, start_field, first, second, edge)
    up, strip = swap(up, "py", 0), swap(strip, "py", 1)
    parts = (shape(*known.shape), shape(*known.shape), shape(KNOWN, 8, LANES))
    known, gap, dist = call(gap_kernel, "gap", parts, start_field, known)
    step = (whole,) * 4 + (sums,)
    u, a0, a1, a2, sent = call(first_kernel, "first_step", step, u, up, strip, gap, dist, alias={0: 0})
    recv = total_over_devices(sent)
    body = lambda *refs: second_kernel(cells, *refs)
    v, b0, b1, b2, sent = call(body, "second_step", step, recv, u, a0, a1, a2, known)
    recv = total_over_devices(sent)
    body = lambda *refs: third_kernel(cells, *refs)
    scratch = [pltpu.VMEM(whole.shape, F32)]
    field, residual = call(body, "finish", (own, own), recv, v, b0, b1, b2, scratch=scratch)
    return field, residual


def solution(mesh):
    placed = (P("px", "py", None), P(None, "px", "py", None))
    return jax.shard_map(
        local,
        mesh=mesh,
        in_specs=placed,
        out_specs=(P("px", "py", None), P("px", "py", None)),
        check_vma=False,
    )
```

```python
import jax
import jax.numpy as jnp
from jax import lax
from jax.experimental import pallas as pl
from jax.experimental.pallas import tpu as pltpu
from jax.sharding import PartitionSpec as P

EPS = 1e-06
DEFLATE = 4.0
ITERS = 3
KNOWN = 8
AXES = ("px", "py")
HX = 7
HY = 8
LANES = 128
F32 = jnp.float32

DIST, CROSS = 8, 16


def iotas():
    row = lax.broadcasted_iota(jnp.int32, (8, LANES), 0)
    lane = lax.broadcasted_iota(jnp.int32, (8, LANES), 1)
    return row, lane


def plane_sums(ref, x, tiles):
    row, lane = iotas()
    top, ncol = ref.shape[1] // 8, ref.shape[2] // LANES
    zero = jnp.zeros((8, LANES), F32)
    need = range(max(tiles[0] - 1, 0), min(tiles[-1] + 2, top))
    v = {(t, c): ref[(x, *tile(t, c))] for t in need for c in range(ncol)}
    up = {(t, c): pltpu.roll(v[t, c], 1, 0) for t in need if t <= tiles[-1] for c in range(ncol)}
    down = {(t, c): pltpu.roll(v[t, c], 7, 0) for t in need if t >= tiles[0] for c in range(ncol)}
    for t in tiles:
        left = [zero] + [pltpu.roll(v[t, c], 1, 1) for c in range(ncol)]
        right = [pltpu.roll(v[t, c], LANES - 1, 1) for c in range(ncol)] + [zero]
        for c in range(ncol):
            a = up[t, c] if t == 0 else jnp.where(row == 0, up[t - 1, c], up[t, c])
            b = down[t, c] if t == top - 1 else jnp.where(row == 7, down[t + 1, c], down[t, c])
            l = jnp.where(lane == 0, left[c], left[c + 1])
            r = jnp.where(lane == LANES - 1, right[c + 1], right[c])
            where = tile(t, c)
            total = (ref[(x - 1, *where)] + ref[(x + 1, *where)]) + (a + b) + (l + r)
            yield t, c, v[t, c], total


def tile(t, c):
    return slice(8 * t, 8 * t + 8), slice(LANES * c, LANES * c + LANES)


def edges():
    ix, iy = lax.axis_index("px"), lax.axis_index("py")
    nx, ny = lax.axis_size("px"), lax.axis_size("py")
    flag = lambda cond: jnp.where(cond, 0.0, 1.0).astype(F32)
    return flag(ix == 0), flag(ix == nx - 1), flag(iy == 0), flag(iy == ny - 1)


def krylov(u_ref, w_refs, q_ref, lo, hi, known_ref, gap, sums_ref):
    planes, top, ncol = u_ref.shape[0], u_ref.shape[1] // 8, u_ref.shape[2] // LANES
    x_lo, x_hi, y_lo, y_hi = edges()
    first, last = HX, planes - HX

    def mask(x, t):
        along = x_lo if x < first else x_hi if x >= last else None
        across = y_lo if t == 0 else y_hi if t == top - 1 else None
        if along is None or across is None:
            return across if along is None else along
        return along * across

    own = range(HY // 8, top - HY // 8)
    for k in range(ITERS):
        src, dst = u_ref if k == 0 else w_refs[k - 1], w_refs[k]
        for x in range(lo + k, hi - k):
            tiles = own if x in (lo + k, hi - k - 1) else range(top)
            for t, c, v, total in plane_sums(src, x, tiles):
                where = (x, *tile(t, c))
                if k == 0:
                    square = v * v
                    q_ref[where] = 2.0 - 6.0 * square
                    value = total - v * (4.0 + 2.0 * square)
                else:
                    value = total + q_ref[where] * v
                m = mask(x, t)
                dst[where] = value if m is None else value * m
    zero = jnp.zeros((8, LANES), F32)
    mus = [zero] * 8
    more = [zero] * (KNOWN * (ITERS + 1))
    if gap is not None:
        more[:KNOWN] = [gap[1][i] for i in range(KNOWN)]
    for x in range(first, last):
        for t, c, w2, total in plane_sums(w_refs[2], x, own):
            q, w0, w1 = (ref[(x, *tile(t, c))] for ref in (q_ref, w_refs[0], w_refs[1]))
            w3 = total + q * w2
            pairs = ((w0, w0), (w0, w1), (w1, w1), (w1, w2), (w2, w2), (w2, w3), (w3, w3))
            for n, (p, q) in enumerate(pairs):
                mus[n] = mus[n] + p * q
    for x in range(first, last):
        for t in own:
            for c in range(ncol):
                u, *ws = (ref[(x, *tile(t, c))] for ref in (u_ref, *w_refs))
                for i in range(KNOWN):
                    where = (i, x - first, *tile(t - HY // 8, c))
                    if gap is None:
                        d = u - known_ref[where]
                        more[i] = more[i] + d * d
                    else:
                        d = gap[0][where]
                    for m in range(ITERS):
                        n = KNOWN * (m + 1) + i
                        more[n] = more[n] + d * ws[m]
    block = jnp.concatenate([jnp.sum(a, axis=0, keepdims=True) for a in (*mus, *more)], axis=0)
    totals = jnp.sum(block, axis=1, keepdims=True)
    hit = lax.broadcasted_iota(jnp.int32, block.shape, 0) == lax.broadcasted_iota(jnp.int32, block.shape, 1)
    line = jnp.sum(jnp.where(hit, totals, 0.0), axis=0, keepdims=True)
    sums_ref[...] = jnp.broadcast_to(line, sums_ref.shape)


def coefficients(recv_ref, cells):
    line = jnp.sum(recv_ref[...], axis=0, keepdims=True)
    line = jnp.broadcast_to(line, (8, LANES))
    mu = [jnp.broadcast_to(line[:, n:n + 1], (8, LANES)) for n in range(7)]
    zero = jnp.zeros((8, LANES), F32)

    def inner(p, q):
        total = None
        for i, a in enumerate(p):
            if a is None:
                continue
            part = None
            for j, b in enumerate(q):
                if b is None:
                    continue
                term = b * mu[i + j]
                part = term if part is None else part + term
            part = a * part
            total = part if total is None else total + part
        return total

    beta = jnp.sqrt(0.25 * mu[0] + EPS)
    basis = [[-0.5 / beta]]
    hess = {}
    for k in range(ITERS):
        vec = basis[k]
        image = [None] * (k + 2)
        for i in range(k + 2):
            a = 0.5 * vec[i - 1] if i > 0 else None
            b = -3.0 * vec[i] if i <= k else None
            image[i] = b if a is None else (a if b is None else a + b)
        for j in range(k + 1):
            hess[j, k] = inner(basis[j], image)
        rest = list(image)
        for j in range(k + 1):
            for i in range(len(basis[j])):
                rest[i] = rest[i] - hess[j, k] * basis[j][i]
        square = jnp.maximum(inner(rest, rest), 0.0)
        hess[k + 1, k] = jnp.sqrt(square + EPS)
        if k < ITERS - 1:
            scale = 1.0 / hess[k + 1, k]
            basis.append([a * scale for a in rest])

    def normal(i, j):
        total = None
        for r in range(ITERS + 1):
            if (r, i) in hess and (r, j) in hess:
                term = hess[r, i] * hess[r, j]
                total = term if total is None else total + term
        return total

    lower = {}
    for j in range(ITERS):
        diag = normal(j, j)
        for r in range(j):
            diag = diag - lower[j, r] * lower[j, r]
        lower[j, j] = jnp.sqrt(diag)
        for i in range(j + 1, ITERS):
            off = normal(i, j)
            for r in range(j):
                off = off - lower[i, r] * lower[j, r]
            lower[i, j] = off / lower[j, j]
    forward = []
    for i in range(ITERS):
        part = beta * hess[0, i]
        for j in range(i):
            part = part - lower[i, j] * forward[j]
        forward.append(part / lower[i, i])
    back = [None] * ITERS
    for i in reversed(range(ITERS)):
        part = forward[i]
        for j in range(i + 1, ITERS):
            part = part - lower[j, i] * back[j]
        back[i] = part / lower[i, i]
    coef = []
    for m in range(ITERS):
        total = zero
        for j in range(m, ITERS):
            total = total + back[j] * basis[j][m]
        coef.append(total)
    lane = lax.broadcasted_iota(jnp.int32, (8, LANES), 1)
    dist = pltpu.roll(line, LANES - DIST, 1)
    dot = zero
    for m in range(ITERS):
        dot = dot + coef[m] * pltpu.roll(line, LANES - CROSS - KNOWN * m, 1)
    mean = dist / cells + EPS
    weight = 1.0 / mean + DEFLATE
    terms = jnp.where(lane < KNOWN, 2.0 * dot / (cells * mean * mean * weight), 0.0)
    total = jnp.sum(terms, axis=1, keepdims=True)
    tau = 1.0 / (1.0 + jnp.abs(jnp.broadcast_to(total, (8, LANES))))
    return [tau * a for a in coef]


def update(u_ref, w_refs, coef, dst, lo, hi, out_ref=None):
    top, ncol = u_ref.shape[1] // 8, u_ref.shape[2] // LANES
    own = range(HY // 8, top - HY // 8)
    for x in range(lo, hi):
        for t in own if x in (lo, hi - 1) else range(top):
            for c in range(ncol):
                where = (x, *tile(t, c))
                value = u_ref[where]
                for a, w in zip(coef, w_refs):
                    value = value + a * w[where]
                dst[where] = value
                if out_ref is not None and t in own and HX <= x < u_ref.shape[0] - HX:
                    out_ref[(x - HX, *tile(t - HY // 8, c))] = value


def parity(axis):
    return lax.axis_index(axis) % 2


def gap_kernel(field_ref, known_ref, out_ref, gap_ref, dist_ref):
    count, bx, by, bz = known_ref.shape
    for i in range(count):
        total = None
        for x in range(bx):
            for t in range(by // 8):
                for c in range(bz // LANES):
                    where = tile(t, c)
                    k = known_ref[(i, x, *where)]
                    d = field_ref[(x, *where)] - k
                    out_ref[(i, x, *where)] = k
                    gap_ref[(i, x, *where)] = d
                    total = d * d if total is None else total + d * d
        dist_ref[i] = total


SHARED = ((1, 6, 5), (2, 5, 4), (3, 4, 6))


def shared_planes(planes):
    for n, (d, rows, other) in enumerate(SHARED):
        yield 2 * n, HX - d, HX - other, rows
        yield 2 * n + 1, planes - 1 - HX + d, planes - 1 - HX + other, rows


def pack_rows(u_ref, out_ref, high):
    planes, rows, bz = u_ref.shape
    bx = planes - 2 * HX
    start = pl.multiple_of(jnp.where(high, rows - 2 * HY, HY), HY)
    out_ref[0:bx] = u_ref[HX:HX + bx, pl.ds(start, HY)]
    row, _ = iotas()
    depth = jnp.where(high, HY - 1 - row, row)
    for n, x, y, count in shared_planes(planes):
        for c in range(bz // LANES):
            cols = slice(LANES * c, LANES * c + LANES)
            a, b = (u_ref[p, pl.ds(start, HY), cols] for p in (x, y))
            b = jnp.where(high, pltpu.roll(b, HY - count, 0), pltpu.roll(b, count, 0))
            out_ref[bx + n, :, cols] = jnp.where(depth < count, a, b)


def unpack_rows(in_ref, u_ref, high):
    planes, rows, bz = u_ref.shape
    bx = planes - 2 * HX
    start = pl.multiple_of(jnp.where(high, rows - HY, 0), HY)
    u_ref[HX:HX + bx, pl.ds(start, HY)] = in_ref[0:bx]
    for n, x, y, count in shared_planes(planes):
        for c in range(bz // LANES):
            cols = slice(LANES * c, LANES * c + LANES)
            both = in_ref[bx + n, :, cols]
            u_ref[x, pl.ds(start, HY), cols] = both
            other = jnp.where(high, pltpu.roll(both, HY - count, 0), pltpu.roll(both, count, 0))
            u_ref[y, pl.ds(start, HY), cols] = other


def place_kernel(own_ref, u_ref):
    bx, by, bz = own_ref.shape
    planes = u_ref.shape[0]
    u_ref[HX:HX + bx, HY:HY + by] = own_ref[...]
    edge = jnp.zeros((1, HY, bz), F32)
    for x in (0, planes - 1):
        for y in (0, HY + by):
            u_ref[x:x + 1, y:y + HY] = edge


def join_kernel(mid_ref, first_ref, second_ref, u_ref, first_out, second_out):
    bx, by, bz = first_ref.shape
    mine = slice(HY, HY + by)
    odd = parity("px")
    u_ref[pl.ds((1 - odd) * (HX + bx), HX), mine] = first_ref[pl.ds(odd * (bx - HX), HX)]
    u_ref[pl.ds(odd * (HX + bx), HX), mine] = second_ref[pl.ds((1 - odd) * (bx - HX), HX)]
    odd = parity("py")
    pack_rows(u_ref, first_out, odd == 0)
    pack_rows(u_ref, second_out, odd == 1)


def first_kernel(mid_ref, first_ref, second_ref, gap_ref, dist_ref, u_ref, w0, w1, w2, sums_ref, q_ref):
    planes = u_ref.shape[0]
    odd = parity("py")
    unpack_rows(first_ref, u_ref, odd == 0)
    unpack_rows(second_ref, u_ref, odd == 1)
    krylov(u_ref, (w0, w1, w2), q_ref, 1, planes - 1, None, (gap_ref, dist_ref), sums_ref)


def second_kernel(cells, recv_ref, u_ref, a0, a1, a2, known_ref, v_ref, w0, w1, w2, sums_ref, q_ref):
    coef = coefficients(recv_ref, cells)
    planes = u_ref.shape[0]
    update(u_ref, (a0, a1, a2), coef, v_ref, 3, planes - 3)
    krylov(v_ref, (w0, w1, w2), q_ref, 4, planes - 4, known_ref, None, sums_ref)


def third_kernel(cells, recv_ref, u_ref, a0, a1, a2, out_hbm, res_hbm, v_ref, out_ref, res_ref, sems):
    coef = coefficients(recv_ref, cells)
    planes, top = u_ref.shape[0], u_ref.shape[1] // 8
    update(u_ref, (a0, a1, a2), coef, v_ref, HX - 1, planes - HX + 1, out_ref)
    field_copy = pltpu.make_async_copy(out_ref, out_hbm, sems.at[0])
    field_copy.start()
    for x in range(HX, planes - HX):
        for t, c, v, total in plane_sums(v_ref, x, range(HY // 8, top - HY // 8)):
            res_ref[(x - HX, *tile(t - HY // 8, c))] = 0.5 * total - v * (2.0 + v * v)
    residual_copy = pltpu.make_async_copy(res_ref, res_hbm, sems.at[1])
    residual_copy.start()
    field_copy.wait()
    residual_copy.wait()


def total_over_devices(rows):
    count = rows.shape[0]
    rows = rows.reshape(count, 1, LANES)
    return lax.all_to_all(rows, AXES, 0, 0).reshape(count, LANES)


def swap(part, axis, first):
    pairs = []
    for i in range(first, lax.axis_size(axis) - 1, 2):
        pairs += [(i, i + 1), (i + 1, i)]
    return lax.ppermute(part, axis, pairs)


def local(start_field, known):
    bx, by, bz = start_field.shape
    devices = lax.axis_size("px") * lax.axis_size("py")
    cells = float(bx * by * bz * devices)
    vmem = pl.BlockSpec(memory_space=pltpu.VMEM)
    params = pltpu.CompilerParams(vmem_limit_bytes=24 * 2**20)
    shape = lambda *dims: jax.ShapeDtypeStruct(dims, F32)

    def call(body, name, outs, *args, scratch=(), alias={}, space=pltpu.VMEM):
        return pl.pallas_call(
            body,
            out_shape=outs,
            in_specs=[vmem] * len(args),
            out_specs=tuple(pl.BlockSpec(memory_space=space) for _ in outs),
            scratch_shapes=scratch,
            input_output_aliases=alias,
            compiler_params=params,
            name=name,
        )(*args)

    planes, rows = bx + 2 * HX, by + 2 * HY
    own, whole = shape(bx, by, bz), shape(planes, rows, bz)
    sums = shape(devices, LANES)
    room = pltpu.VMEM(whole.shape, F32)
    first, second = swap(start_field, "px", 0), swap(start_field, "px", 1)
    strip = shape(bx + 2 * len(SHARED), HY, bz)
    (u,) = call(place_kernel, "place", (whole,), start_field)
    u, first, second = call(join_kernel, "join", (whole, strip, strip), u, first, second, alias={0: 0})
    first, second = swap(first, "py", 0), swap(second, "py", 1)
    parts = (shape(*known.shape), shape(*known.shape), shape(KNOWN, 8, LANES))
    known, gap, dist = call(gap_kernel, "gap", parts, start_field, known)
    step = (whole,) * 4 + (sums,)
    u, a0, a1, a2, sent = call(
        first_kernel, "first_step", step, u, first, second, gap, dist, scratch=[room], alias={0: 0}
    )
    recv = total_over_devices(sent)
    body = lambda *refs: second_kernel(cells, *refs)
    v, b0, b1, b2, sent = call(body, "second_step", step, recv, u, a0, a1, a2, known, scratch=[room])
    recv = total_over_devices(sent)
    body = lambda *refs: third_kernel(cells, *refs)
    scratch = [room, pltpu.VMEM(own.shape, F32), pltpu.VMEM(own.shape, F32), pltpu.SemaphoreType.DMA((2,))]
    field, residual = call(body, "finish", (own, own), recv, v, b0, b1, b2, scratch=scratch, space=pl.ANY)
    return field, residual


def solution(mesh):
    placed = (P("px", "py", None), P(None, "px", "py", None))
    return jax.shard_map(
        local,
        mesh=mesh,
        in_specs=placed,
        out_specs=(P("px", "py", None), P("px", "py", None)),
        check_vma=False,
    )
```

```python
import jax
import jax.numpy as jnp
from jax import lax
from jax.experimental import pallas as pl
from jax.experimental.pallas import tpu as pltpu
from jax.sharding import PartitionSpec as P

EPS = 1e-06
DEFLATE = 4.0
ITERS = 3
KNOWN = 8
AXES = ("px", "py")
HX = 7
HY = 8
LANES = 128
F32 = jnp.float32

DIST, CROSS = 8, 16


def iotas():
    row = lax.broadcasted_iota(jnp.int32, (8, LANES), 0)
    lane = lax.broadcasted_iota(jnp.int32, (8, LANES), 1)
    return row, lane


def plane_sums(ref, x, tiles):
    row, lane = iotas()
    top, ncol = ref.shape[1] // 8, ref.shape[2] // LANES
    zero = jnp.zeros((8, LANES), F32)
    need = range(max(tiles[0] - 1, 0), min(tiles[-1] + 2, top))
    v = {(t, c): ref[(x, *tile(t, c))] for t in need for c in range(ncol)}
    up = {(t, c): pltpu.roll(v[t, c], 1, 0) for t in need if t <= tiles[-1] for c in range(ncol)}
    down = {(t, c): pltpu.roll(v[t, c], 7, 0) for t in need if t >= tiles[0] for c in range(ncol)}
    for t in tiles:
        left = [zero] + [pltpu.roll(v[t, c], 1, 1) for c in range(ncol)]
        right = [pltpu.roll(v[t, c], LANES - 1, 1) for c in range(ncol)] + [zero]
        for c in range(ncol):
            a = up[t, c] if t == 0 else jnp.where(row == 0, up[t - 1, c], up[t, c])
            b = down[t, c] if t == top - 1 else jnp.where(row == 7, down[t + 1, c], down[t, c])
            l = jnp.where(lane == 0, left[c], left[c + 1])
            r = jnp.where(lane == LANES - 1, right[c + 1], right[c])
            where = tile(t, c)
            total = (ref[(x - 1, *where)] + ref[(x + 1, *where)]) + (a + b) + (l + r)
            yield t, c, v[t, c], total


def tile(t, c):
    return slice(8 * t, 8 * t + 8), slice(LANES * c, LANES * c + LANES)


def edges():
    ix, iy = lax.axis_index("px"), lax.axis_index("py")
    nx, ny = lax.axis_size("px"), lax.axis_size("py")
    flag = lambda cond: jnp.where(cond, 0.0, 1.0).astype(F32)
    return flag(ix == 0), flag(ix == nx - 1), flag(iy == 0), flag(iy == ny - 1)


def krylov(u_ref, w_refs, q_ref, lo, hi, known_ref, gap, sums_ref):
    planes, top, ncol = u_ref.shape[0], u_ref.shape[1] // 8, u_ref.shape[2] // LANES
    x_lo, x_hi, y_lo, y_hi = edges()
    first, last = HX, planes - HX

    def mask(x, t):
        along = x_lo if x < first else x_hi if x >= last else None
        across = y_lo if t == 0 else y_hi if t == top - 1 else None
        if along is None or across is None:
            return across if along is None else along
        return along * across

    own = range(HY // 8, top - HY // 8)
    for k in range(ITERS):
        src, dst = u_ref if k == 0 else w_refs[k - 1], w_refs[k]
        for x in range(lo + k, hi - k):
            tiles = own if x in (lo + k, hi - k - 1) else range(top)
            for t, c, v, total in plane_sums(src, x, tiles):
                where = (x, *tile(t, c))
                if k == 0:
                    square = v * v
                    q_ref[where] = 2.0 - 6.0 * square
                    value = total - v * (4.0 + 2.0 * square)
                else:
                    value = total + q_ref[where] * v
                m = mask(x, t)
                dst[where] = value if m is None else value * m
    zero = jnp.zeros((8, LANES), F32)
    mus = [zero] * 8
    more = [zero] * (KNOWN * (ITERS + 1))
    if gap is not None:
        more[:KNOWN] = [gap[1][i] for i in range(KNOWN)]
    for x in range(first, last):
        for t, c, w2, total in plane_sums(w_refs[2], x, own):
            q, w0, w1 = (ref[(x, *tile(t, c))] for ref in (q_ref, w_refs[0], w_refs[1]))
            w3 = total + q * w2
            pairs = ((w0, w0), (w0, w1), (w1, w1), (w1, w2), (w2, w2), (w2, w3), (w3, w3))
            for n, (p, q) in enumerate(pairs):
                mus[n] = mus[n] + p * q
    for x in range(first, last):
        for t in own:
            for c in range(ncol):
                u, *ws = (ref[(x, *tile(t, c))] for ref in (u_ref, *w_refs))
                for i in range(KNOWN):
                    where = (i, x - first, *tile(t - HY // 8, c))
                    if gap is None:
                        d = u - known_ref[where]
                        more[i] = more[i] + d * d
                    else:
                        d = gap[0][where]
                    for m in range(ITERS):
                        n = KNOWN * (m + 1) + i
                        more[n] = more[n] + d * ws[m]
    block = jnp.concatenate([jnp.sum(a, axis=0, keepdims=True) for a in (*mus, *more)], axis=0)
    totals = jnp.sum(block, axis=1, keepdims=True)
    hit = lax.broadcasted_iota(jnp.int32, block.shape, 0) == lax.broadcasted_iota(jnp.int32, block.shape, 1)
    line = jnp.sum(jnp.where(hit, totals, 0.0), axis=0, keepdims=True)
    sums_ref[...] = jnp.broadcast_to(line, sums_ref.shape)


def coefficients(recv_ref, cells):
    line = jnp.sum(recv_ref[...], axis=0, keepdims=True)
    line = jnp.broadcast_to(line, (8, LANES))
    mu = [jnp.broadcast_to(line[:, n:n + 1], (8, LANES)) for n in range(7)]
    zero = jnp.zeros((8, LANES), F32)

    def inner(p, q):
        total = None
        for i, a in enumerate(p):
            if a is None:
                continue
            part = None
            for j, b in enumerate(q):
                if b is None:
                    continue
                term = b * mu[i + j]
                part = term if part is None else part + term
            part = a * part
            total = part if total is None else total + part
        return total

    beta = jnp.sqrt(0.25 * mu[0] + EPS)
    basis = [[-0.5 / beta]]
    hess = {}
    for k in range(ITERS):
        vec = basis[k]
        image = [None] * (k + 2)
        for i in range(k + 2):
            a = 0.5 * vec[i - 1] if i > 0 else None
            b = -3.0 * vec[i] if i <= k else None
            image[i] = b if a is None else (a if b is None else a + b)
        for j in range(k + 1):
            hess[j, k] = inner(basis[j], image)
        rest = list(image)
        for j in range(k + 1):
            for i in range(len(basis[j])):
                rest[i] = rest[i] - hess[j, k] * basis[j][i]
        square = jnp.maximum(inner(rest, rest), 0.0)
        hess[k + 1, k] = jnp.sqrt(square + EPS)
        if k < ITERS - 1:
            scale = 1.0 / hess[k + 1, k]
            basis.append([a * scale for a in rest])

    def normal(i, j):
        total = None
        for r in range(ITERS + 1):
            if (r, i) in hess and (r, j) in hess:
                term = hess[r, i] * hess[r, j]
                total = term if total is None else total + term
        return total

    lower = {}
    for j in range(ITERS):
        diag = normal(j, j)
        for r in range(j):
            diag = diag - lower[j, r] * lower[j, r]
        lower[j, j] = jnp.sqrt(diag)
        for i in range(j + 1, ITERS):
            off = normal(i, j)
            for r in range(j):
                off = off - lower[i, r] * lower[j, r]
            lower[i, j] = off / lower[j, j]
    forward = []
    for i in range(ITERS):
        part = beta * hess[0, i]
        for j in range(i):
            part = part - lower[i, j] * forward[j]
        forward.append(part / lower[i, i])
    back = [None] * ITERS
    for i in reversed(range(ITERS)):
        part = forward[i]
        for j in range(i + 1, ITERS):
            part = part - lower[j, i] * back[j]
        back[i] = part / lower[i, i]
    coef = []
    for m in range(ITERS):
        total = zero
        for j in range(m, ITERS):
            total = total + back[j] * basis[j][m]
        coef.append(total)
    lane = lax.broadcasted_iota(jnp.int32, (8, LANES), 1)
    dist = pltpu.roll(line, LANES - DIST, 1)
    dot = zero
    for m in range(ITERS):
        dot = dot + coef[m] * pltpu.roll(line, LANES - CROSS - KNOWN * m, 1)
    mean = dist / cells + EPS
    weight = 1.0 / mean + DEFLATE
    terms = jnp.where(lane < KNOWN, 2.0 * dot / (cells * mean * mean * weight), 0.0)
    total = jnp.sum(terms, axis=1, keepdims=True)
    tau = 1.0 / (1.0 + jnp.abs(jnp.broadcast_to(total, (8, LANES))))
    return [tau * a for a in coef]


def update(u_ref, w_refs, coef, dst, lo, hi, out_ref=None):
    top, ncol = u_ref.shape[1] // 8, u_ref.shape[2] // LANES
    own = range(HY // 8, top - HY // 8)
    for x in range(lo, hi):
        for t in own if x in (lo, hi - 1) else range(top):
            for c in range(ncol):
                where = (x, *tile(t, c))
                value = u_ref[where]
                for a, w in zip(coef, w_refs):
                    value = value + a * w[where]
                dst[where] = value
                if out_ref is not None and t in own and HX <= x < u_ref.shape[0] - HX:
                    out_ref[(x - HX, *tile(t - HY // 8, c))] = value


def parity(axis):
    return lax.axis_index(axis) % 2


def gap_kernel(field_ref, known_ref, out_ref, gap_ref, dist_ref):
    count, bx, by, bz = known_ref.shape
    for i in range(count):
        total = None
        for x in range(bx):
            for t in range(by // 8):
                for c in range(bz // LANES):
                    where = tile(t, c)
                    k = known_ref[(i, x, *where)]
                    d = field_ref[(x, *where)] - k
                    out_ref[(i, x, *where)] = k
                    gap_ref[(i, x, *where)] = d
                    total = d * d if total is None else total + d * d
        dist_ref[i] = total


SHARED = ((1, 6, 5), (2, 5, 4), (3, 4, 6))


def shared_planes(planes):
    for n, (d, rows, other) in enumerate(SHARED):
        yield 2 * n, HX - d, HX - other, rows
        yield 2 * n + 1, planes - 1 - HX + d, planes - 1 - HX + other, rows


def pack_rows(u_ref, out_ref, high):
    planes, rows, bz = u_ref.shape
    bx = planes - 2 * HX
    start = pl.multiple_of(jnp.where(high, rows - 2 * HY, HY), HY)
    out_ref[0:bx] = u_ref[HX:HX + bx, pl.ds(start, HY)]
    row, _ = iotas()
    depth = jnp.where(high, HY - 1 - row, row)
    for n, x, y, count in shared_planes(planes):
        for c in range(bz // LANES):
            cols = slice(LANES * c, LANES * c + LANES)
            a, b = (u_ref[p, pl.ds(start, HY), cols] for p in (x, y))
            b = jnp.where(high, pltpu.roll(b, HY - count, 0), pltpu.roll(b, count, 0))
            out_ref[bx + n, :, cols] = jnp.where(depth < count, a, b)


def unpack_rows(in_ref, u_ref, high):
    planes, rows, bz = u_ref.shape
    bx = planes - 2 * HX
    start = pl.multiple_of(jnp.where(high, rows - HY, 0), HY)
    u_ref[HX:HX + bx, pl.ds(start, HY)] = in_ref[0:bx]
    for n, x, y, count in shared_planes(planes):
        for c in range(bz // LANES):
            cols = slice(LANES * c, LANES * c + LANES)
            both = in_ref[bx + n, :, cols]
            u_ref[x, pl.ds(start, HY), cols] = both
            other = jnp.where(high, pltpu.roll(both, HY - count, 0), pltpu.roll(both, count, 0))
            u_ref[y, pl.ds(start, HY), cols] = other


def place_kernel(own_ref, u_ref):
    bx, by, bz = own_ref.shape
    planes = u_ref.shape[0]
    u_ref[HX:HX + bx, HY:HY + by] = own_ref[...]
    edge = jnp.zeros((1, HY, bz), F32)
    for x in (0, planes - 1):
        for y in (0, HY + by):
            u_ref[x:x + 1, y:y + HY] = edge


def join_kernel(mid_ref, second_ref, first_ref, u_ref, first_out, second_out):
    bx, by, bz = first_ref.shape
    mine = slice(HY, HY + by)
    odd = parity("px")
    u_ref[pl.ds((1 - odd) * (HX + bx), HX), mine] = first_ref[pl.ds(odd * (bx - HX), HX)]
    u_ref[pl.ds(odd * (HX + bx), HX), mine] = second_ref[pl.ds((1 - odd) * (bx - HX), HX)]
    odd = parity("py")
    pack_rows(u_ref, first_out, odd == 0)
    pack_rows(u_ref, second_out, odd == 1)


def first_kernel(mid_ref, second_ref, first_ref, gap_ref, dist_ref, u_ref, w0, w1, w2, sums_ref, q_ref):
    planes = u_ref.shape[0]
    odd = parity("py")
    unpack_rows(first_ref, u_ref, odd == 0)
    unpack_rows(second_ref, u_ref, odd == 1)
    krylov(u_ref, (w0, w1, w2), q_ref, 1, planes - 1, None, (gap_ref, dist_ref), sums_ref)


def second_kernel(cells, recv_ref, u_ref, a0, a1, a2, known_ref, v_ref, w0, w1, w2, sums_ref, q_ref):
    coef = coefficients(recv_ref, cells)
    planes = u_ref.shape[0]
    update(u_ref, (a0, a1, a2), coef, v_ref, 3, planes - 3)
    krylov(v_ref, (w0, w1, w2), q_ref, 4, planes - 4, known_ref, None, sums_ref)


def third_kernel(cells, recv_ref, u_ref, a0, a1, a2, out_hbm, res_hbm, v_ref, out_ref, res_ref, sems):
    coef = coefficients(recv_ref, cells)
    planes, top = u_ref.shape[0], u_ref.shape[1] // 8
    update(u_ref, (a0, a1, a2), coef, v_ref, HX - 1, planes - HX + 1, out_ref)
    field_copy = pltpu.make_async_copy(out_ref, out_hbm, sems.at[0])
    field_copy.start()
    for x in range(HX, planes - HX):
        for t, c, v, total in plane_sums(v_ref, x, range(HY // 8, top - HY // 8)):
            res_ref[(x - HX, *tile(t - HY // 8, c))] = 0.5 * total - v * (2.0 + v * v)
    residual_copy = pltpu.make_async_copy(res_ref, res_hbm, sems.at[1])
    residual_copy.start()
    field_copy.wait()
    residual_copy.wait()


def total_over_devices(rows):
    count = rows.shape[0]
    rows = rows.reshape(count, 1, LANES)
    return lax.all_to_all(rows, AXES, 0, 0).reshape(count, LANES)


def swap(part, axis, first):
    pairs = []
    for i in range(first, lax.axis_size(axis) - 1, 2):
        pairs += [(i, i + 1), (i + 1, i)]
    return lax.ppermute(part, axis, pairs)


def local(start_field, known):
    bx, by, bz = start_field.shape
    devices = lax.axis_size("px") * lax.axis_size("py")
    cells = float(bx * by * bz * devices)
    vmem = pl.BlockSpec(memory_space=pltpu.VMEM)
    params = pltpu.CompilerParams(vmem_limit_bytes=24 * 2**20)
    shape = lambda *dims: jax.ShapeDtypeStruct(dims, F32)

    def call(body, name, outs, *args, scratch=(), alias={}, space=pltpu.VMEM):
        return pl.pallas_call(
            body,
            out_shape=outs,
            in_specs=[vmem] * len(args),
            out_specs=tuple(pl.BlockSpec(memory_space=space) for _ in outs),
            scratch_shapes=scratch,
            input_output_aliases=alias,
            compiler_params=params,
            name=name,
        )(*args)

    planes, rows = bx + 2 * HX, by + 2 * HY
    own, whole = shape(bx, by, bz), shape(planes, rows, bz)
    sums = shape(devices, LANES)
    room = pltpu.VMEM(whole.shape, F32)
    second = swap(start_field, "px", 1)
    first = swap(start_field, "px", 0)
    strip = shape(bx + 2 * len(SHARED), HY, bz)
    (u,) = call(place_kernel, "place", (whole,), start_field)
    u, first, second = call(join_kernel, "join", (whole, strip, strip), u, second, first, alias={0: 0})
    second = swap(second, "py", 1)
    first = swap(first, "py", 0)
    parts = (shape(*known.shape), shape(*known.shape), shape(KNOWN, 8, LANES))
    known, gap, dist = call(gap_kernel, "gap", parts, start_field, known)
    step = (whole,) * 4 + (sums,)
    u, a0, a1, a2, sent = call(
        first_kernel, "first_step", step, u, second, first, gap, dist, scratch=[room], alias={0: 0}
    )
    recv = total_over_devices(sent)
    body = lambda *refs: second_kernel(cells, *refs)
    v, b0, b1, b2, sent = call(body, "second_step", step, recv, u, a0, a1, a2, known, scratch=[room])
    recv = total_over_devices(sent)
    body = lambda *refs: third_kernel(cells, *refs)
    scratch = [room, pltpu.VMEM(own.shape, F32), pltpu.VMEM(own.shape, F32), pltpu.SemaphoreType.DMA((2,))]
    field, residual = call(body, "finish", (own, own), recv, v, b0, b1, b2, scratch=scratch, space=pl.ANY)
    return field, residual


def solution(mesh):
    placed = (P("px", "py", None), P(None, "px", "py", None))
    return jax.shard_map(
        local,
        mesh=mesh,
        in_specs=placed,
        out_specs=(P("px", "py", None), P("px", "py", None)),
        check_vma=False,
    )
```

```python
import jax
import jax.numpy as jnp
from jax import lax
from jax.experimental import pallas as pl
from jax.experimental.pallas import tpu as pltpu
from jax.sharding import PartitionSpec as P

EPS = 1e-06
NOISE = 1e-07
DEFLATE = 4.0
ITERS = 3
KNOWN = 8
AXES = ("px", "py")
HX = 7
HY = 8
LANES = 128
F32 = jnp.float32

DIST, CROSS = 8, 16


def iotas():
    row = lax.broadcasted_iota(jnp.int32, (8, LANES), 0)
    lane = lax.broadcasted_iota(jnp.int32, (8, LANES), 1)
    return row, lane


def plane_sums(ref, x, tiles):
    row, lane = iotas()
    top, ncol = ref.shape[1] // 8, ref.shape[2] // LANES
    zero = jnp.zeros((8, LANES), F32)
    need = range(max(tiles[0] - 1, 0), min(tiles[-1] + 2, top))
    v = {(t, c): ref[(x, *tile(t, c))] for t in need for c in range(ncol)}
    up = {(t, c): pltpu.roll(v[t, c], 1, 0) for t in need if t <= tiles[-1] for c in range(ncol)}
    down = {(t, c): pltpu.roll(v[t, c], 7, 0) for t in need if t >= tiles[0] for c in range(ncol)}
    for t in tiles:
        left = [zero] + [pltpu.roll(v[t, c], 1, 1) for c in range(ncol)]
        right = [pltpu.roll(v[t, c], LANES - 1, 1) for c in range(ncol)] + [zero]
        for c in range(ncol):
            a = up[t, c] if t == 0 else jnp.where(row == 0, up[t - 1, c], up[t, c])
            b = down[t, c] if t == top - 1 else jnp.where(row == 7, down[t + 1, c], down[t, c])
            l = jnp.where(lane == 0, left[c], left[c + 1])
            r = jnp.where(lane == LANES - 1, right[c + 1], right[c])
            where = tile(t, c)
            total = (ref[(x - 1, *where)] + ref[(x + 1, *where)]) + (a + b) + (l + r)
            yield t, c, v[t, c], total


def tile(t, c):
    return slice(8 * t, 8 * t + 8), slice(LANES * c, LANES * c + LANES)


def edges():
    ix, iy = lax.axis_index("px"), lax.axis_index("py")
    nx, ny = lax.axis_size("px"), lax.axis_size("py")
    flag = lambda cond: jnp.where(cond, 0.0, 1.0).astype(F32)
    return flag(ix == 0), flag(ix == nx - 1), flag(iy == 0), flag(iy == ny - 1)


def krylov(u_ref, w_refs, q_ref, lo, hi, known_ref, gap, sums_ref):
    planes, top, ncol = u_ref.shape[0], u_ref.shape[1] // 8, u_ref.shape[2] // LANES
    x_lo, x_hi, y_lo, y_hi = edges()
    first, last = HX, planes - HX

    def mask(x, t):
        along = x_lo if x < first else x_hi if x >= last else None
        across = y_lo if t == 0 else y_hi if t == top - 1 else None
        if along is None or across is None:
            return across if along is None else along
        return along * across

    own = range(HY // 8, top - HY // 8)
    for k in range(ITERS):
        src, dst = u_ref if k == 0 else w_refs[k - 1], w_refs[k]
        for x in range(lo + k, hi - k):
            tiles = own if x in (lo + k, hi - k - 1) else range(top)
            for t, c, v, total in plane_sums(src, x, tiles):
                where = (x, *tile(t, c))
                if k == 0:
                    square = v * v
                    q_ref[where] = -1.0 - 6.0 * square
                    value = total - v * (4.0 + 2.0 * square)
                else:
                    value = total + q_ref[where] * v
                m = mask(x, t)
                dst[where] = value if m is None else value * m
    zero = jnp.zeros((8, LANES), F32)
    mus = [zero] * 8
    more = [zero] * (KNOWN * (ITERS + 1))
    if gap is not None:
        more[:KNOWN] = [gap[1][i] for i in range(KNOWN)]
    for x in range(first, last):
        for t, c, w2, total in plane_sums(w_refs[2], x, own):
            q, w0, w1 = (ref[(x, *tile(t, c))] for ref in (q_ref, w_refs[0], w_refs[1]))
            w3 = total + q * w2
            pairs = ((w0, w0), (w0, w1), (w1, w1), (w1, w2), (w2, w2), (w2, w3), (w3, w3))
            for n, (p, q) in enumerate(pairs):
                mus[n] = mus[n] + p * q
    for x in range(first, last):
        for t in own:
            for c in range(ncol):
                u, *ws = (ref[(x, *tile(t, c))] for ref in (u_ref, *w_refs))
                for i in range(KNOWN):
                    where = (i, x - first, *tile(t - HY // 8, c))
                    if gap is None:
                        d = u - known_ref[where]
                        more[i] = more[i] + d * d
                    else:
                        d = gap[0][where]
                    for m in range(ITERS):
                        n = KNOWN * (m + 1) + i
                        more[n] = more[n] + d * ws[m]
    block = jnp.concatenate([jnp.sum(a, axis=0, keepdims=True) for a in (*mus, *more)], axis=0)
    totals = jnp.sum(block, axis=1, keepdims=True)
    hit = lax.broadcasted_iota(jnp.int32, block.shape, 0) == lax.broadcasted_iota(jnp.int32, block.shape, 1)
    line = jnp.sum(jnp.where(hit, totals, 0.0), axis=0, keepdims=True)
    sums_ref[...] = jnp.broadcast_to(line, sums_ref.shape)


def coefficients(recv_ref, cells):
    line = jnp.sum(recv_ref[...], axis=0, keepdims=True)
    line = jnp.broadcast_to(line, (8, LANES))
    mu = [jnp.broadcast_to(line[:, n:n + 1], (8, LANES)) for n in range(7)]
    zero = jnp.zeros((8, LANES), F32)

    size = [jnp.abs(m) for m in mu]

    def inner(p, q, mu=mu):
        total = None
        for i, a in enumerate(p):
            if a is None:
                continue
            part = None
            for j, b in enumerate(q):
                if b is None:
                    continue
                term = b * mu[i + j]
                part = term if part is None else part + term
            part = a * part
            total = part if total is None else total + part
        return total

    beta = jnp.sqrt(0.25 * mu[0] + EPS)
    basis = [[-0.5 / beta]]
    hess = {}
    for k in range(ITERS):
        vec = basis[k]
        image = [None] * (k + 2)
        for i in range(k + 2):
            a = 0.5 * vec[i - 1] if i > 0 else None
            b = -1.5 * vec[i] if i <= k else None
            image[i] = b if a is None else (a if b is None else a + b)
        for j in range(k + 1):
            hess[j, k] = inner(basis[j], image)
        rest = list(image)
        for j in range(k + 1):
            for i in range(len(basis[j])):
                rest[i] = rest[i] - hess[j, k] * basis[j][i]
        square = inner(rest, rest)
        lengths = [jnp.abs(a) for a in rest]
        sound = square > NOISE * inner(lengths, lengths, size)
        square = jnp.where(sound, square, 0.0)
        hess[k + 1, k] = jnp.sqrt(square + EPS)
        if k < ITERS - 1:
            scale = jnp.where(sound, 1.0 / hess[k + 1, k], 0.0)
            basis.append([a * scale for a in rest])

    def normal(i, j):
        total = None
        for r in range(ITERS + 1):
            if (r, i) in hess and (r, j) in hess:
                term = hess[r, i] * hess[r, j]
                total = term if total is None else total + term
        return total

    lower = {}
    for j in range(ITERS):
        diag = normal(j, j)
        for r in range(j):
            diag = diag - lower[j, r] * lower[j, r]
        diag = jnp.maximum(diag, hess[j + 1, j] * hess[j + 1, j])
        lower[j, j] = jnp.sqrt(diag)
        for i in range(j + 1, ITERS):
            off = normal(i, j)
            for r in range(j):
                off = off - lower[i, r] * lower[j, r]
            lower[i, j] = off / lower[j, j]
    forward = []
    for i in range(ITERS):
        part = beta * hess[0, i]
        for j in range(i):
            part = part - lower[i, j] * forward[j]
        forward.append(part / lower[i, i])
    back = [None] * ITERS
    for i in reversed(range(ITERS)):
        part = forward[i]
        for j in range(i + 1, ITERS):
            part = part - lower[j, i] * back[j]
        back[i] = part / lower[i, i]
    coef = []
    for m in range(ITERS):
        total = zero
        for j in range(m, ITERS):
            total = total + back[j] * basis[j][m]
        coef.append(total)
    lane = lax.broadcasted_iota(jnp.int32, (8, LANES), 1)
    dist = pltpu.roll(line, LANES - DIST, 1)
    dot = zero
    for m in range(ITERS):
        dot = dot + coef[m] * pltpu.roll(line, LANES - CROSS - KNOWN * m, 1)
    mean = dist / cells + EPS
    weight = 1.0 / mean + DEFLATE
    terms = jnp.where(lane < KNOWN, 2.0 * dot / (cells * mean * mean * weight), 0.0)
    total = jnp.sum(terms, axis=1, keepdims=True)
    tau = 1.0 / (1.0 + jnp.abs(jnp.broadcast_to(total, (8, LANES))))
    return [tau * a for a in coef]


def update(u_ref, w_refs, coef, dst, lo, hi, out_ref=None):
    top, ncol = u_ref.shape[1] // 8, u_ref.shape[2] // LANES
    own = range(HY // 8, top - HY // 8)
    for x in range(lo, hi):
        for t in own if x in (lo, hi - 1) else range(top):
            for c in range(ncol):
                where = (x, *tile(t, c))
                value = u_ref[where]
                for a, w in zip(coef, w_refs):
                    value = value + a * w[where]
                dst[where] = value
                if out_ref is not None and t in own and HX <= x < u_ref.shape[0] - HX:
                    out_ref[(x - HX, *tile(t - HY // 8, c))] = value


def parity(axis):
    return lax.axis_index(axis) % 2


def gap_kernel(field_ref, known_ref, out_ref, gap_ref, dist_ref):
    count, bx, by, bz = known_ref.shape
    for i in range(count):
        total = None
        for x in range(bx):
            for t in range(by // 8):
                for c in range(bz // LANES):
                    where = tile(t, c)
                    k = known_ref[(i, x, *where)]
                    d = field_ref[(x, *where)] - k
                    out_ref[(i, x, *where)] = k
                    gap_ref[(i, x, *where)] = d
                    total = d * d if total is None else total + d * d
        dist_ref[i] = total


SHARED = ((1, 6, 5), (2, 5, 4), (3, 4, 6))


def shared_planes(planes):
    for n, (d, rows, other) in enumerate(SHARED):
        yield 2 * n, HX - d, HX - other, rows
        yield 2 * n + 1, planes - 1 - HX + d, planes - 1 - HX + other, rows


def pack_rows(u_ref, out_ref, high):
    planes, rows, bz = u_ref.shape
    bx = planes - 2 * HX
    start = pl.multiple_of(jnp.where(high, rows - 2 * HY, HY), HY)
    out_ref[0:bx] = u_ref[HX:HX + bx, pl.ds(start, HY)]
    row, _ = iotas()
    depth = jnp.where(high, HY - 1 - row, row)
    for n, x, y, count in shared_planes(planes):
        for c in range(bz // LANES):
            cols = slice(LANES * c, LANES * c + LANES)
            a, b = (u_ref[p, pl.ds(start, HY), cols] for p in (x, y))
            b = jnp.where(high, pltpu.roll(b, HY - count, 0), pltpu.roll(b, count, 0))
            out_ref[bx + n, :, cols] = jnp.where(depth < count, a, b)


def unpack_rows(in_ref, u_ref, high):
    planes, rows, bz = u_ref.shape
    bx = planes - 2 * HX
    start = pl.multiple_of(jnp.where(high, rows - HY, 0), HY)
    u_ref[HX:HX + bx, pl.ds(start, HY)] = in_ref[0:bx]
    for n, x, y, count in shared_planes(planes):
        for c in range(bz // LANES):
            cols = slice(LANES * c, LANES * c + LANES)
            both = in_ref[bx + n, :, cols]
            u_ref[x, pl.ds(start, HY), cols] = both
            other = jnp.where(high, pltpu.roll(both, HY - count, 0), pltpu.roll(both, count, 0))
            u_ref[y, pl.ds(start, HY), cols] = other


def place_kernel(own_ref, u_ref):
    bx, by, bz = own_ref.shape
    planes = u_ref.shape[0]
    u_ref[HX:HX + bx, HY:HY + by] = own_ref[...]
    edge = jnp.zeros((1, HY, bz), F32)
    for x in (0, planes - 1):
        for y in (0, HY + by):
            u_ref[x:x + 1, y:y + HY] = edge


def join_kernel(mid_ref, second_ref, first_ref, u_ref, first_out, second_out):
    bx, by, bz = first_ref.shape
    mine = slice(HY, HY + by)
    odd = parity("px")
    u_ref[pl.ds((1 - odd) * (HX + bx), HX), mine] = first_ref[pl.ds(odd * (bx - HX), HX)]
    u_ref[pl.ds(odd * (HX + bx), HX), mine] = second_ref[pl.ds((1 - odd) * (bx - HX), HX)]
    odd = parity("py")
    pack_rows(u_ref, first_out, odd == 0)
    pack_rows(u_ref, second_out, odd == 1)


def first_kernel(mid_ref, second_ref, first_ref, gap_ref, dist_ref, u_ref, w0, w1, w2, sums_ref, q_ref):
    planes = u_ref.shape[0]
    odd = parity("py")
    unpack_rows(first_ref, u_ref, odd == 0)
    unpack_rows(second_ref, u_ref, odd == 1)
    krylov(u_ref, (w0, w1, w2), q_ref, 1, planes - 1, None, (gap_ref, dist_ref), sums_ref)


def second_kernel(cells, recv_ref, u_ref, a0, a1, a2, known_ref, v_ref, w0, w1, w2, sums_ref, q_ref):
    coef = coefficients(recv_ref, cells)
    planes = u_ref.shape[0]
    update(u_ref, (a0, a1, a2), coef, v_ref, 3, planes - 3)
    krylov(v_ref, (w0, w1, w2), q_ref, 4, planes - 4, known_ref, None, sums_ref)


def third_kernel(cells, recv_ref, u_ref, a0, a1, a2, out_hbm, res_hbm, v_ref, out_ref, res_ref, sems):
    coef = coefficients(recv_ref, cells)
    planes, top = u_ref.shape[0], u_ref.shape[1] // 8
    update(u_ref, (a0, a1, a2), coef, v_ref, HX - 1, planes - HX + 1, out_ref)
    field_copy = pltpu.make_async_copy(out_ref, out_hbm, sems.at[0])
    field_copy.start()
    for x in range(HX, planes - HX):
        for t, c, v, total in plane_sums(v_ref, x, range(HY // 8, top - HY // 8)):
            res_ref[(x - HX, *tile(t - HY // 8, c))] = 0.5 * total - v * (2.0 + v * v)
    residual_copy = pltpu.make_async_copy(res_ref, res_hbm, sems.at[1])
    residual_copy.start()
    field_copy.wait()
    residual_copy.wait()


def total_over_devices(rows):
    count = rows.shape[0]
    rows = rows.reshape(count, 1, LANES)
    return lax.all_to_all(rows, AXES, 0, 0).reshape(count, LANES)


def swap(part, axis, first):
    pairs = []
    for i in range(first, lax.axis_size(axis) - 1, 2):
        pairs += [(i, i + 1), (i + 1, i)]
    return lax.ppermute(part, axis, pairs)


def local(start_field, known):
    bx, by, bz = start_field.shape
    devices = lax.axis_size("px") * lax.axis_size("py")
    cells = float(bx * by * bz * devices)
    vmem = pl.BlockSpec(memory_space=pltpu.VMEM)
    params = pltpu.CompilerParams(vmem_limit_bytes=24 * 2**20)
    shape = lambda *dims: jax.ShapeDtypeStruct(dims, F32)

    def call(body, name, outs, *args, scratch=(), alias={}, space=pltpu.VMEM):
        return pl.pallas_call(
            body,
            out_shape=outs,
            in_specs=[vmem] * len(args),
            out_specs=tuple(pl.BlockSpec(memory_space=space) for _ in outs),
            scratch_shapes=scratch,
            input_output_aliases=alias,
            compiler_params=params,
            name=name,
        )(*args)

    planes, rows = bx + 2 * HX, by + 2 * HY
    own, whole = shape(bx, by, bz), shape(planes, rows, bz)
    sums = shape(devices, LANES)
    room = pltpu.VMEM(whole.shape, F32)
    second = swap(start_field, "px", 1)
    first = swap(start_field, "px", 0)
    strip = shape(bx + 2 * len(SHARED), HY, bz)
    (u,) = call(place_kernel, "place", (whole,), start_field)
    u, first, second = call(join_kernel, "join", (whole, strip, strip), u, second, first, alias={0: 0})
    second = swap(second, "py", 1)
    first = swap(first, "py", 0)
    parts = (shape(*known.shape), shape(*known.shape), shape(KNOWN, 8, LANES))
    known, gap, dist = call(gap_kernel, "gap", parts, start_field, known)
    step = (whole,) * 4 + (sums,)
    u, a0, a1, a2, sent = call(
        first_kernel, "first_step", step, u, second, first, gap, dist, scratch=[room], alias={0: 0}
    )
    recv = total_over_devices(sent)
    body = lambda *refs: second_kernel(cells, *refs)
    v, b0, b1, b2, sent = call(body, "second_step", step, recv, u, a0, a1, a2, known, scratch=[room])
    recv = total_over_devices(sent)
    body = lambda *refs: third_kernel(cells, *refs)
    scratch = [room, pltpu.VMEM(own.shape, F32), pltpu.VMEM(own.shape, F32), pltpu.SemaphoreType.DMA((2,))]
    field, residual = call(body, "finish", (own, own), recv, v, b0, b1, b2, scratch=scratch, space=pl.ANY)
    return field, residual


def solution(mesh):
    placed = (P("px", "py", None), P(None, "px", "py", None))
    return jax.shard_map(
        local,
        mesh=mesh,
        in_specs=placed,
        out_specs=(P("px", "py", None), P("px", "py", None)),
        check_vma=False,
    )
```

```python
import jax
import jax.numpy as jnp
from jax import lax
from jax.experimental import pallas as pl
from jax.experimental.pallas import tpu as pltpu
from jax.sharding import PartitionSpec as P

EPS = 1e-06
NOISE = 1e-07
DEFLATE = 4.0
ITERS = 3
KNOWN = 8
AXES = ("px", "py")
HX = 7
HY = 8
LANES = 128
F32 = jnp.float32

DIST, CROSS = 8, 16


def iotas():
    row = lax.broadcasted_iota(jnp.int32, (8, LANES), 0)
    lane = lax.broadcasted_iota(jnp.int32, (8, LANES), 1)
    return row, lane


def plane_sums(ref, x, tiles):
    row, lane = iotas()
    top, ncol = ref.shape[1] // 8, ref.shape[2] // LANES
    zero = jnp.zeros((8, LANES), F32)
    need = range(max(tiles[0] - 1, 0), min(tiles[-1] + 2, top))
    v = {(t, c): ref[(x, *tile(t, c))] for t in need for c in range(ncol)}
    up = {(t, c): pltpu.roll(v[t, c], 1, 0) for t in need if t <= tiles[-1] for c in range(ncol)}
    down = {(t, c): pltpu.roll(v[t, c], 7, 0) for t in need if t >= tiles[0] for c in range(ncol)}
    for t in tiles:
        left = [zero] + [pltpu.roll(v[t, c], 1, 1) for c in range(ncol)]
        right = [pltpu.roll(v[t, c], LANES - 1, 1) for c in range(ncol)] + [zero]
        for c in range(ncol):
            a = up[t, c] if t == 0 else jnp.where(row == 0, up[t - 1, c], up[t, c])
            b = down[t, c] if t == top - 1 else jnp.where(row == 7, down[t + 1, c], down[t, c])
            l = jnp.where(lane == 0, left[c], left[c + 1])
            r = jnp.where(lane == LANES - 1, right[c + 1], right[c])
            where = tile(t, c)
            total = (ref[(x - 1, *where)] + ref[(x + 1, *where)]) + (a + b) + (l + r)
            yield t, c, v[t, c], total


def tile(t, c):
    return slice(8 * t, 8 * t + 8), slice(LANES * c, LANES * c + LANES)


def edges():
    ix, iy = lax.axis_index("px"), lax.axis_index("py")
    nx, ny = lax.axis_size("px"), lax.axis_size("py")
    flag = lambda cond: jnp.where(cond, 0.0, 1.0).astype(F32)
    return flag(ix == 0), flag(ix == nx - 1), flag(iy == 0), flag(iy == ny - 1)


def krylov(u_ref, w_refs, q_ref, lo, hi, known_ref, gap, sums_ref):
    planes, top, ncol = u_ref.shape[0], u_ref.shape[1] // 8, u_ref.shape[2] // LANES
    x_lo, x_hi, y_lo, y_hi = edges()
    first, last = HX, planes - HX

    def mask(x, t):
        along = x_lo if x < first else x_hi if x >= last else None
        across = y_lo if t == 0 else y_hi if t == top - 1 else None
        if along is None or across is None:
            return across if along is None else along
        return along * across

    own = range(HY // 8, top - HY // 8)
    for k in range(ITERS):
        src, dst = u_ref if k == 0 else w_refs[k - 1], w_refs[k]
        for x in range(lo + k, hi - k):
            tiles = own if x in (lo + k, hi - k - 1) else range(top)
            for t, c, v, total in plane_sums(src, x, tiles):
                where = (x, *tile(t, c))
                if k == 0:
                    square = v * v
                    q_ref[where] = -1.0 - 6.0 * square
                    value = total - v * (4.0 + 2.0 * square)
                else:
                    value = total + q_ref[where] * v
                m = mask(x, t)
                dst[where] = value if m is None else value * m
    zero = jnp.zeros((8, LANES), F32)
    mus = [zero] * 8
    more = [zero] * (KNOWN * (ITERS + 1))
    if gap is not None:
        more[:KNOWN] = [gap[1][i] for i in range(KNOWN)]
    for x in range(first, last):
        for t, c, w2, total in plane_sums(w_refs[2], x, own):
            q, w0, w1 = (ref[(x, *tile(t, c))] for ref in (q_ref, w_refs[0], w_refs[1]))
            w3 = total + q * w2
            pairs = ((w0, w0), (w0, w1), (w1, w1), (w1, w2), (w2, w2), (w2, w3), (w3, w3))
            for n, (p, q) in enumerate(pairs):
                mus[n] = mus[n] + p * q
    for x in range(first, last):
        for t in own:
            for c in range(ncol):
                u, *ws = (ref[(x, *tile(t, c))] for ref in (u_ref, *w_refs))
                for i in range(KNOWN):
                    where = (i, x - first, *tile(t - HY // 8, c))
                    if gap is None:
                        d = u - known_ref[where]
                        more[i] = more[i] + d * d
                    else:
                        d = gap[0][where]
                    for m in range(ITERS):
                        n = KNOWN * (m + 1) + i
                        more[n] = more[n] + d * ws[m]
    block = jnp.concatenate([jnp.sum(a, axis=0, keepdims=True) for a in (*mus, *more)], axis=0)
    totals = jnp.sum(block, axis=1, keepdims=True)
    hit = lax.broadcasted_iota(jnp.int32, block.shape, 0) == lax.broadcasted_iota(jnp.int32, block.shape, 1)
    line = jnp.sum(jnp.where(hit, totals, 0.0), axis=0, keepdims=True)
    sums_ref[...] = jnp.broadcast_to(line, sums_ref.shape)


def coefficients(recv_ref, cells):
    line = jnp.sum(recv_ref[...], axis=0, keepdims=True)
    line = jnp.broadcast_to(line, (8, LANES))
    mu = [jnp.broadcast_to(line[:, n:n + 1], (8, LANES)) for n in range(7)]
    zero = jnp.zeros((8, LANES), F32)

    size = [jnp.abs(m) for m in mu]

    def inner(p, q, mu=mu):
        total = None
        for i, a in enumerate(p):
            if a is None:
                continue
            part = None
            for j, b in enumerate(q):
                if b is None:
                    continue
                term = b * mu[i + j]
                part = term if part is None else part + term
            part = a * part
            total = part if total is None else total + part
        return total

    beta = jnp.sqrt(0.25 * mu[0] + EPS)
    basis = [[-0.5 / beta]]
    hess = {}
    for k in range(ITERS):
        vec = basis[k]
        image = [None] * (k + 2)
        for i in range(k + 2):
            a = 0.5 * vec[i - 1] if i > 0 else None
            b = -1.5 * vec[i] if i <= k else None
            image[i] = b if a is None else (a if b is None else a + b)
        for j in range(k + 1):
            hess[j, k] = inner(basis[j], image)
        rest = list(image)
        for j in range(k + 1):
            for i in range(len(basis[j])):
                rest[i] = rest[i] - hess[j, k] * basis[j][i]
        square = inner(rest, rest)
        lengths = [jnp.abs(a) for a in rest]
        sound = square > NOISE * inner(lengths, lengths, size)
        square = jnp.where(sound, square, 0.0)
        hess[k + 1, k] = jnp.sqrt(square + EPS)
        if k < ITERS - 1:
            scale = jnp.where(sound, 1.0 / hess[k + 1, k], 0.0)
            basis.append([a * scale for a in rest])

    def normal(i, j):
        total = None
        for r in range(ITERS + 1):
            if (r, i) in hess and (r, j) in hess:
                term = hess[r, i] * hess[r, j]
                total = term if total is None else total + term
        return total

    lower = {}
    for j in range(ITERS):
        diag = normal(j, j)
        for r in range(j):
            diag = diag - lower[j, r] * lower[j, r]
        diag = jnp.maximum(diag, hess[j + 1, j] * hess[j + 1, j])
        lower[j, j] = jnp.sqrt(diag)
        for i in range(j + 1, ITERS):
            off = normal(i, j)
            for r in range(j):
                off = off - lower[i, r] * lower[j, r]
            lower[i, j] = off / lower[j, j]
    forward = []
    for i in range(ITERS):
        part = beta * hess[0, i]
        for j in range(i):
            part = part - lower[i, j] * forward[j]
        forward.append(part / lower[i, i])
    back = [None] * ITERS
    for i in reversed(range(ITERS)):
        part = forward[i]
        for j in range(i + 1, ITERS):
            part = part - lower[j, i] * back[j]
        back[i] = part / lower[i, i]
    coef = []
    for m in range(ITERS):
        total = zero
        for j in range(m, ITERS):
            total = total + back[j] * basis[j][m]
        coef.append(total)
    lane = lax.broadcasted_iota(jnp.int32, (8, LANES), 1)
    dist = pltpu.roll(line, LANES - DIST, 1)
    dot = zero
    for m in range(ITERS):
        dot = dot + coef[m] * pltpu.roll(line, LANES - CROSS - KNOWN * m, 1)
    mean = dist / cells + EPS
    weight = 1.0 / mean + DEFLATE
    terms = jnp.where(lane < KNOWN, 2.0 * dot / (cells * mean * mean * weight), 0.0)
    total = jnp.sum(terms, axis=1, keepdims=True)
    tau = 1.0 / (1.0 + jnp.abs(jnp.broadcast_to(total, (8, LANES))))
    return [tau * a for a in coef]


def update(u_ref, w_refs, coef, dst, lo, hi, out_ref=None):
    top, ncol = u_ref.shape[1] // 8, u_ref.shape[2] // LANES
    own = range(HY // 8, top - HY // 8)
    for x in range(lo, hi):
        for t in own if x in (lo, hi - 1) else range(top):
            for c in range(ncol):
                where = (x, *tile(t, c))
                value = u_ref[where]
                for a, w in zip(coef, w_refs):
                    value = value + a * w[where]
                dst[where] = value
                if out_ref is not None and t in own and HX <= x < u_ref.shape[0] - HX:
                    out_ref[(x - HX, *tile(t - HY // 8, c))] = value


def parity(axis):
    return lax.axis_index(axis) % 2


def gap_kernel(field_ref, known_ref, out_ref, gap_ref, dist_ref):
    count, bx, by, bz = known_ref.shape
    for i in range(count):
        total = None
        for x in range(bx):
            for t in range(by // 8):
                for c in range(bz // LANES):
                    where = tile(t, c)
                    k = known_ref[(i, x, *where)]
                    d = field_ref[(x, *where)] - k
                    out_ref[(i, x, *where)] = k
                    gap_ref[(i, x, *where)] = d
                    total = d * d if total is None else total + d * d
        dist_ref[i] = total


SHARED = ((1, 6, 5), (2, 5, 4), (3, 4, 6))


def shared_planes(planes):
    for n, (d, rows, other) in enumerate(SHARED):
        yield 2 * n, HX - d, HX - other, rows
        yield 2 * n + 1, planes - 1 - HX + d, planes - 1 - HX + other, rows


def pack_rows(u_ref, out_ref, high, base):
    planes, rows, bz = u_ref.shape
    start = pl.multiple_of(jnp.where(high, rows - 2 * HY, HY), HY)
    if base:
        out_ref[0:base] = u_ref[HX:HX + base, pl.ds(start, HY)]
    row, _ = iotas()
    depth = jnp.where(high, HY - 1 - row, row)
    for n, x, y, count in shared_planes(planes):
        for c in range(bz // LANES):
            cols = slice(LANES * c, LANES * c + LANES)
            a, b = (u_ref[p, pl.ds(start, HY), cols] for p in (x, y))
            b = jnp.where(high, pltpu.roll(b, HY - count, 0), pltpu.roll(b, count, 0))
            out_ref[base + n, :, cols] = jnp.where(depth < count, a, b)


def unpack_rows(in_ref, u_ref, high, base):
    planes, rows, bz = u_ref.shape
    start = pl.multiple_of(jnp.where(high, rows - HY, 0), HY)
    if base:
        u_ref[HX:HX + base, pl.ds(start, HY)] = in_ref[0:base]
    for n, x, y, count in shared_planes(planes):
        for c in range(bz // LANES):
            cols = slice(LANES * c, LANES * c + LANES)
            both = in_ref[base + n, :, cols]
            u_ref[x, pl.ds(start, HY), cols] = both
            other = jnp.where(high, pltpu.roll(both, HY - count, 0), pltpu.roll(both, count, 0))
            u_ref[y, pl.ds(start, HY), cols] = other


def edge_kernel(field_ref, rows_ref):
    by = field_ref.shape[1]
    start = pl.multiple_of(parity("py") * (by - HY), HY)
    rows_ref[...] = field_ref[:, pl.ds(start, HY)]


def place_kernel(own_ref, u_ref):
    bx, by, bz = own_ref.shape
    planes = u_ref.shape[0]
    u_ref[HX:HX + bx, HY:HY + by] = own_ref[...]
    edge = jnp.zeros((1, HY, bz), F32)
    for x in (0, planes - 1):
        for y in (0, HY + by):
            u_ref[x:x + 1, y:y + HY] = edge


def join_kernel(mid_ref, first_ref, second_ref, rows_ref, u_ref, first_out, second_out):
    bx, by, bz = first_ref.shape
    mine = slice(HY, HY + by)
    odd = parity("px")
    u_ref[pl.ds((1 - odd) * (HX + bx), HX), mine] = first_ref[pl.ds(odd * (bx - HX), HX)]
    u_ref[pl.ds(odd * (HX + bx), HX), mine] = second_ref[pl.ds((1 - odd) * (bx - HX), HX)]
    odd = parity("py")
    u_ref[HX:HX + bx, pl.ds(pl.multiple_of(odd * (HY + by), HY), HY)] = rows_ref[...]
    pack_rows(u_ref, first_out, odd == 0, bx)
    pack_rows(u_ref, second_out, odd == 1, 0)


def first_kernel(mid_ref, first_ref, second_ref, gap_ref, dist_ref, u_ref, w0, w1, w2, sums_ref, q_ref):
    planes = u_ref.shape[0]
    odd = parity("py")
    unpack_rows(first_ref, u_ref, odd == 0, planes - 2 * HX)
    unpack_rows(second_ref, u_ref, odd == 1, 0)
    krylov(u_ref, (w0, w1, w2), q_ref, 1, planes - 1, None, (gap_ref, dist_ref), sums_ref)


def second_kernel(cells, recv_ref, u_ref, a0, a1, a2, known_ref, v_ref, w0, w1, w2, sums_ref, q_ref):
    coef = coefficients(recv_ref, cells)
    planes = u_ref.shape[0]
    update(u_ref, (a0, a1, a2), coef, v_ref, 3, planes - 3)
    krylov(v_ref, (w0, w1, w2), q_ref, 4, planes - 4, known_ref, None, sums_ref)


def third_kernel(cells, recv_ref, u_ref, a0, a1, a2, out_hbm, res_hbm, v_ref, out_ref, res_ref, sems):
    coef = coefficients(recv_ref, cells)
    planes, top = u_ref.shape[0], u_ref.shape[1] // 8
    update(u_ref, (a0, a1, a2), coef, v_ref, HX - 1, planes - HX + 1, out_ref)
    field_copy = pltpu.make_async_copy(out_ref, out_hbm, sems.at[0])
    field_copy.start()
    for x in range(HX, planes - HX):
        for t, c, v, total in plane_sums(v_ref, x, range(HY // 8, top - HY // 8)):
            res_ref[(x - HX, *tile(t - HY // 8, c))] = 0.5 * total - v * (2.0 + v * v)
    residual_copy = pltpu.make_async_copy(res_ref, res_hbm, sems.at[1])
    residual_copy.start()
    field_copy.wait()
    residual_copy.wait()


def total_over_devices(rows):
    count = rows.shape[0]
    rows = rows.reshape(count, 1, LANES)
    return lax.all_to_all(rows, AXES, 0, 0).reshape(count, LANES)


def swap(part, axis, first):
    pairs = []
    for i in range(first, lax.axis_size(axis) - 1, 2):
        pairs += [(i, i + 1), (i + 1, i)]
    return lax.ppermute(part, axis, pairs)


def local(start_field, known):
    bx, by, bz = start_field.shape
    devices = lax.axis_size("px") * lax.axis_size("py")
    cells = float(bx * by * bz * devices)
    vmem = pl.BlockSpec(memory_space=pltpu.VMEM)
    params = pltpu.CompilerParams(vmem_limit_bytes=24 * 2**20)
    shape = lambda *dims: jax.ShapeDtypeStruct(dims, F32)

    def call(body, name, outs, *args, scratch=(), alias={}, space=pltpu.VMEM):
        return pl.pallas_call(
            body,
            out_shape=outs,
            in_specs=[vmem] * len(args),
            out_specs=tuple(pl.BlockSpec(memory_space=space) for _ in outs),
            scratch_shapes=scratch,
            input_output_aliases=alias,
            compiler_params=params,
            name=name,
        )(*args)

    planes, rows = bx + 2 * HX, by + 2 * HY
    own, whole = shape(bx, by, bz), shape(planes, rows, bz)
    sums = shape(devices, LANES)
    room = pltpu.VMEM(whole.shape, F32)
    first = swap(start_field, "px", 0)
    second = swap(start_field, "px", 1)
    (rows_out,) = call(edge_kernel, "edge", (shape(bx, HY, bz),), start_field)
    rows_in = swap(rows_out, "py", 1)
    side, strip = shape(bx + 2 * len(SHARED), HY, bz), shape(2 * len(SHARED), HY, bz)
    (u,) = call(place_kernel, "place", (whole,), start_field)
    u, first, second = call(join_kernel, "join", (whole, side, strip), u, first, second, rows_in, alias={0: 0})
    first = swap(first, "py", 0)
    second = swap(second, "py", 1)
    parts = (shape(*known.shape), shape(*known.shape), shape(KNOWN, 8, LANES))
    known, gap, dist = call(gap_kernel, "gap", parts, start_field, known)
    step = (whole,) * 4 + (sums,)
    u, a0, a1, a2, sent = call(
        first_kernel, "first_step", step, u, first, second, gap, dist, scratch=[room], alias={0: 0}
    )
    recv = total_over_devices(sent)
    body = lambda *refs: second_kernel(cells, *refs)
    v, b0, b1, b2, sent = call(body, "second_step", step, recv, u, a0, a1, a2, known, scratch=[room])
    recv = total_over_devices(sent)
    body = lambda *refs: third_kernel(cells, *refs)
    scratch = [room, pltpu.VMEM(own.shape, F32), pltpu.VMEM(own.shape, F32), pltpu.SemaphoreType.DMA((2,))]
    field, residual = call(body, "finish", (own, own), recv, v, b0, b1, b2, scratch=scratch, space=pl.ANY)
    return field, residual


def solution(mesh):
    placed = (P("px", "py", None), P(None, "px", "py", None))
    return jax.shard_map(
        local,
        mesh=mesh,
        in_specs=placed,
        out_specs=(P("px", "py", None), P("px", "py", None)),
        check_vma=False,
    )
```
